256 devices in a mesh: seq: 64 (over y, z, core), tab: 4 (over x).
Axes of the slice: x: 4, y: 4, z: 8, core: 2. Of those that a mesh axis runs over, the one named last changes fastest.
Arguments:
- cotangent: bfloat16 [65536, 2560], P('seq', 'tab'), may hold values from -6 to 6
- saved_value: bfloat16 [65536, 2560], P('seq', 'tab'), may hold values from -6 to 6
- gate_scale: float32 [65536], P('seq'), may hold values from 0.2 to 1
- conv_weight: float32 [4, 2560], P(None, 'tab'), may hold values from -3 to 3
- value_weight: bfloat16 [1280, 2560], P(None, 'tab'), may hold values from -0.25 to 0.25
- owner_ids: int32 [8, 65536, 1], P('tab', 'seq'), may hold values from 0 to 63; in each aligned block of 1024 rows (0 to 1023, 1024 to 2047, ..., all dimensions but the last counted through in order) at most 64 rows name the same one
- local_row: int32 [8, 65536], P('tab', 'seq'), may hold values from 0 to 511
- row_table: float32 [8, 32768, 160], P('tab', 'seq'), may hold values from -6 to 6
- moment_one: float32 [8, 32768, 160], P('tab', 'seq'), may hold values from -6 to 6
- moment_two: float32 [8, 32768, 160], P('tab', 'seq'), may hold values from 0.5 to 4
Outputs:
- new_table: float32 [8, 32768, 160], P('tab', 'seq')
- new_first: float32 [8, 32768, 160], P('tab', 'seq')
- new_second: float32 [8, 32768, 160], P('tab', 'seq')
The draws below stay inside these ranges and needn't reach their ends.
Inputs may be any that keep to these rules, and one draw needn't show every extreme that they name: `owner_ids`: within each aligned block of 1024 tokens of one head (one device's tokens), no owner is named by more than 64 tokens; in some blocks one owner is named by exactly 64.
All inputs are finite; a program needn't handle non-finite values.
Results may differ from the reference program's by a relative error of at most 0.0029.
Values may be sent and summed in bfloat16 or wider, within the bound.
No kernel may reach another device: no remote copies, remote signals or barrier semaphores. Data moves between devices by JAX's collectives and lax.ppermute only.
A program may use at most 128 MiB of HBM per device.

```python
import math
import jax
import jax.numpy as jnp
import numpy as np

D = 2560
HEADS = 8
HEAD_DIM = 160
TOK_DEV = 1024
ROWS_OWN = 512
MEM = 1280
TOKENS = 65536
ROWS = 32768
CAP = 64
N_SEQ = 64


def with_ends(values, own_key, smallest, largest):
    longest = values.shape.index(max(values.shape))
    spots = []
    for shift in (0, 1):
        where = [jax.random.randint(jax.random.fold_in(own_key, axis), (), 0, length) for axis, length in enumerate(values.shape)]
        where[longest] = (where[longest] + shift) % values.shape[longest]
        spots.append(tuple(where))
    return values.at[spots[0]].set(smallest).at[spots[1]].set(largest)


def spiked(array, key, source, target, shards_of, factor):
    owner, partner = [(jnp.arange(array.shape[axis_at]) // (array.shape[axis_at] // shards_of)).reshape([-1 if axis == axis_at else 1 for axis in range(array.ndim)]) for axis_at in (source, target)]
    chosen = jax.random.permutation(key, shards_of)[partner]
    strong = (owner == chosen) | (owner == (partner + shards_of // 2) % shards_of)
    return jnp.where(strong, factor * array, array)


def shard_levels(key, dims, shards, least, largest):
    gain, own = 1.0, jax.random.fold_in(key, 6)
    for position, shards_of in shards:
        steps = jnp.exp(jax.random.uniform(jax.random.fold_in(own, position), (shards_of,), jnp.float32, least / len(shards), largest / len(shards)))
        gain = gain * jnp.repeat(steps, dims[position] // shards_of).reshape([-1 if axis == position else 1 for axis in range(len(dims))])
    return gain


def rank_table(number_of, slope):
    portions = [(1 << 20) // math.isqrt(rank ** slope) + 1 for rank in range(1, number_of + 1)]
    width = 1 + sum(portions) // (1 << 30)
    return np.cumsum(np.array([max(1, weight // width) for weight in portions]))


def skewed_ids(rng, dims, count, skew):
    grid = rank_table(count, skew)
    lot = jax.random.randint(jax.random.fold_in(rng, 1), dims, 0, int(grid[count - 1]))
    rank = jnp.searchsorted(jnp.asarray(grid, jnp.int32), lot, side="right")
    return jax.random.permutation(jax.random.fold_in(rng, 2), count)[rank].astype(jnp.int32)


def assign_block(key, own, number, rows, count, top, bound, slope):
    order = jax.random.permutation(key, count)
    heavy_load, usual = portions_of(count, rows * top, bound, slope, True), portions_of(count, rows * top, bound, slope, False)
    places = jnp.arange(count)

    def named(lengths, offset_by):
        used = int((lengths > 0).sum())
        fixed = max(1, used // 4)
        shifted = fixed + (places - fixed + offset_by * (used - fixed)) % max(1, count - fixed)
        return jnp.zeros((count,), jnp.int32).at[order[jnp.where(places < fixed, places, shifted)]].set(jnp.asarray(lengths, jnp.int32))

    lengths = jnp.where(number % 4 == 0, named(heavy_load, number // 4), named(usual, number - number // 4 - 1))
    mixed = jax.random.permutation(jax.random.fold_in(own, 3), count)
    giver, sink = mixed[0:count // 2 * 2:2], mixed[1:count // 2 * 2:2]
    room = jnp.minimum(lengths[giver] - 1, bound - lengths[sink]) // 2
    room = jnp.where((giver == order[0]) | (sink == order[0]) | (lengths[sink] == 0), 0, jnp.maximum(room, 0))
    shifted = jax.random.randint(jax.random.fold_in(own, 4), (count // 2,), 0, 1 << 20) % (room + 1)
    lengths = lengths.at[giver].add(-shifted).at[sink].add(shifted)
    labels = jnp.searchsorted(jnp.cumsum(lengths), jnp.arange(rows * top), side="right").astype(jnp.int32)
    grid = labels.reshape(top, rows).T
    grid = grid[jax.random.permutation(jax.random.fold_in(own, 1), rows)]
    offset_by = jax.random.randint(jax.random.fold_in(own, 2), (rows, 1), 0, top)
    return jnp.take_along_axis(grid, (jnp.arange(top)[None, :] + offset_by) % top, axis=1)


def portions_of(number_of, total, bound, lean, full):
    loads = [(1 << 20) // math.isqrt(standing ** lean) + 1 for standing in range(1, number_of + 1)]
    largest = bound if full else min(bound, max(-(-total // number_of), total * loads[0] // sum(loads)))
    least = 1 if total - largest >= number_of - 1 else 0
    given, rest = [largest] + [least] * (number_of - 1), total - largest - least * (number_of - 1)
    while rest > 0:
        movable = [i for i in range(1, number_of) if given[i] < largest] or [i for i in range(1, number_of) if given[i] < bound]
        pool, budget = sum([loads[i] for i in movable]), rest
        for i in movable:
            extra = min(bound - given[i], max(1, budget * loads[i] // pool), rest)
            given[i] = given[i] + extra
            rest = rest - extra
    return np.array(given)


def normal_values(own_key, extent, width, most, split=(), held_as=jnp.bfloat16):
    result = jax.random.normal(own_key, extent, jnp.float32) * width
    if len(split) > 0:
        result = shard_levels(own_key, extent, split, -0.22, 0.18) * result
    return jnp.clip(result, min=-most, max=most).astype(held_as)


def bell_draw_with(own_key, shape, deviation, reach, shards, heavy, kind=jnp.bfloat16):
    entries = deviation * jax.random.normal(own_key, shape, jnp.float32)
    if shards:
        entries = entries * shard_levels(own_key, shape, shards, -0.22, 0.18)
    return jnp.clip(spiked(entries, jax.random.fold_in(own_key, 3), *heavy), -reach, reach).astype(kind)


def setup_inputs(seed: int = 0) -> dict:
    arg_keys = jax.random.split(jax.random.key(seed), 11)
    cotangent = normal_values(arg_keys[0], (TOKENS, D), 1.0, 6.0, ((0, 64), (1, 4)))
    saved_value = normal_values(arg_keys[1], (TOKENS, D), 1.0, 6.0, ((0, 64), (1, 4)))
    gate_scale = jnp.clip(0.2 + 0.8 * jax.random.uniform(arg_keys[2], (TOKENS,), jnp.float32) ** shard_levels(arg_keys[2], (TOKENS,), ((0, 64),), -0.2, 0.2), 0.2, 1.0)
    conv_weight = normal_values(arg_keys[3], (4, D), 0.5, 3.0, ((1, 4),), jnp.float32)
    value_weight = bell_draw_with(arg_keys[4], (MEM, D), MEM ** -0.5, 0.25, ((1, 4),), (1, 0, 4, 2.0))
    owner_ids_keys = jax.random.split(jax.random.fold_in(arg_keys[5], 1), HEADS * TOKENS // TOK_DEV)
    owner_ids_turns = jax.random.permutation(jax.random.fold_in(arg_keys[5], 3), HEADS * TOKENS // TOK_DEV)
    owner_ids = jax.vmap(lambda own, number: assign_block(jax.random.fold_in(arg_keys[5], 2), own, number, TOK_DEV, N_SEQ, 1, CAP, 2))(owner_ids_keys, owner_ids_turns).reshape((HEADS, TOKENS, 1))
    local_row = with_ends(skewed_ids(arg_keys[6], (HEADS, TOKENS), ROWS_OWN, 2), jax.random.fold_in(arg_keys[6], 3), 0, ROWS_OWN - 1).astype(jnp.int32)
    row_table = normal_values(arg_keys[7], (HEADS, ROWS, HEAD_DIM), 1.0, 6.0, ((0, 4), (1, 64)), jnp.float32)
    moment_one = normal_values(arg_keys[8], (HEADS, ROWS, HEAD_DIM), 1.0, 6.0, ((0, 4), (1, 64)), jnp.float32)
    moment_two = jnp.clip(jnp.exp(math.log(4.0) - 2.0794415 * jax.random.uniform(arg_keys[9], (HEADS, ROWS, HEAD_DIM), jnp.float32) ** shard_levels(arg_keys[9], (HEADS, ROWS, HEAD_DIM), ((0, 4), (1, 64)), -0.2, 0.2)), 0.5, 4.0)
    return dict(cotangent=cotangent, saved_value=saved_value, gate_scale=gate_scale, conv_weight=conv_weight, value_weight=value_weight, owner_ids=owner_ids, local_row=local_row, row_table=row_table, moment_one=moment_one, moment_two=moment_two)


beta_one = 0.9
beta_two = 0.95
learn_rate = 0.01
adam_steps = 10.0
epsilon = 1e-08

def reference(cotangent, saved_value, gate_scale, conv_weight, value_weight, owner_ids, local_row, row_table, moment_one, moment_two):
    tokens = cotangent.shape[0]
    upstream = cotangent.astype(jnp.float32)
    value_rows = saved_value.astype(jnp.float32)
    padded_value = jnp.pad(value_rows, ((9, 0), (0, 0)))
    mixed_conv = jnp.zeros(upstream.shape, jnp.float32)
    for tap_index in range(4):
        row_start = 9 - 3 * tap_index
        mixed_conv = mixed_conv + conv_weight[tap_index][None, :] * padded_value[row_start:row_start + tokens]
    squashed = jax.nn.sigmoid(mixed_conv)
    conv_grad = upstream * squashed * (1.0 + mixed_conv * (1.0 - squashed))
    padded_grad = jnp.pad(conv_grad, ((0, 9), (0, 0)))
    value_grad = upstream
    for tap_index in range(4):
        row_start = 3 * tap_index
        value_grad = value_grad + conv_weight[tap_index][None, :] * padded_grad[row_start:row_start + tokens]
    scaled = (gate_scale[:, None] * value_grad).astype(jnp.bfloat16)
    memory_grad = jnp.dot(scaled, value_weight.T, preferred_element_type=jnp.float32)
    heads_grad = jnp.transpose(memory_grad.reshape(tokens, HEADS, HEAD_DIM), (1, 0, 2))
    row_ids = (owner_ids[:, :, 0] * ROWS_OWN + local_row).astype(jnp.int32)
    head_ids = jnp.broadcast_to(jnp.arange(HEADS, dtype=jnp.int32)[:, None], row_ids.shape)
    row_grad = jnp.zeros(row_table.shape, jnp.float32).at[head_ids, row_ids].add(heads_grad)
    row_hits = jnp.zeros(row_table.shape[:2], jnp.int32).at[head_ids, row_ids].add(1)
    touched = (row_hits > 0)[:, :, None]
    first_next = beta_one * moment_one + (1.0 - beta_one) * row_grad
    second_next = beta_two * moment_two + (1.0 - beta_two) * row_grad * row_grad
    update = first_next / (1.0 - beta_one ** adam_steps) / (jnp.sqrt(second_next / (1.0 - beta_two ** adam_steps)) + epsilon)
    table_next = row_table - learn_rate * update
    return (jnp.where(touched, table_next, row_table), jnp.where(touched, first_next, moment_one), jnp.where(touched, second_next, moment_two))
```

```python
import jax
import jax.numpy as jnp
from jax import lax
from jax.experimental import pallas as pl
from jax.experimental.pallas import tpu as pltpu
from jax.sharding import PartitionSpec as P

beta_one = 0.9
beta_two = 0.95
learn_rate = 0.01
adam_steps = 10.0
epsilon = 1e-08

LANES = 128
HALO = 16
DIGIT = 32
META = 8


def shift_by(block, axis, distance, wrap):
    size = lax.axis_size(axis)
    if wrap:
        route = [(i, (i + distance) % size) for i in range(size)]
    else:
        route = [(i, i + distance) for i in range(size) if 0 <= i + distance < size]
    return lax.ppermute(block, axis, route)


def whole(shape, dtype):
    return jax.ShapeDtypeStruct(shape, dtype)


def slot_kernel(owners_ref, slot_ref, *, peers, cap):
    heads, length = owners_ref.shape
    owner_of = lax.broadcasted_iota(jnp.int32, (peers, LANES), 0)
    before = lax.broadcasted_iota(jnp.int32, (LANES, 2 * LANES), 0)
    after = lax.broadcasted_iota(jnp.int32, (LANES, 2 * LANES), 1)
    counter = jnp.where((before < after) | (after >= LANES), 1.0, 0.0).astype(jnp.bfloat16)
    carry = jnp.zeros((heads * peers, LANES), jnp.float32)
    for block in range(length // LANES):
        lanes = slice(block * LANES, (block + 1) * LANES)
        named = [
            jnp.where(owners_ref[h : h + 1, lanes] == owner_of, 1.0, 0.0) for h in range(heads)
        ]
        named = jnp.concatenate(named, axis=0)
        counts = jnp.dot(
            named.astype(jnp.bfloat16), counter, preferred_element_type=jnp.float32
        )
        rank = named * (counts[:, :LANES] + carry)
        carry = carry + counts[:, LANES:]
        for h in range(heads):
            own = jnp.sum(rank[h * peers : (h + 1) * peers], axis=0, keepdims=True)
            slot_ref[h : h + 1, lanes] = owners_ref[h : h + 1, lanes] * cap + own.astype(jnp.int32)


def slots_of(owners, peers, cap):
    return pl.pallas_call(
        lambda *refs: slot_kernel(*refs, peers=peers, cap=cap),
        out_shape=whole(owners.shape, jnp.int32),
        name="slots",
    )(owners)


def adjoint_kernel(
    tab_ref, cot_ref, value_ref, prior_ref, next_value_ref, next_cot_ref, gate_ref, taps_ref,
    weight_ref, *refs, pieces, heads, head_dim, tabs
):
    outs, (value_pad, grad_pad, scaled) = refs[:-3], refs[-3:]
    length, width = cot_ref.shape
    strips = width // LANES
    rows = LANES
    for strip in range(strips):
        lanes = slice(strip * LANES, (strip + 1) * LANES)
        value_pad[strip, :HALO] = prior_ref[:, lanes].astype(jnp.float32)
        value_pad[strip, HALO : HALO + length] = value_ref[:, lanes].astype(jnp.float32)
        value_pad[strip, HALO + length :] = next_value_ref[:, lanes].astype(jnp.float32)

    def adjoint(strip, start, count, upstream):
        lanes = slice(strip * LANES, (strip + 1) * LANES)
        mixed = taps_ref[0:1, lanes] * value_pad[strip, pl.ds(start + HALO, count)]
        for tap in range(1, 4):
            mixed = mixed + taps_ref[tap : tap + 1, lanes] * value_pad[
                strip, pl.ds(start + HALO - 3 * tap, count)
            ]
        squashed = jax.nn.sigmoid(mixed)
        return upstream * squashed * (1.0 + mixed * (1.0 - squashed))

    def first(block, carry):
        start = pl.multiple_of(block * rows, rows)
        for strip in range(strips):
            lanes = slice(strip * LANES, (strip + 1) * LANES)
            upstream = cot_ref[pl.ds(start, rows), lanes].astype(jnp.float32)
            grad_pad[strip, pl.ds(start, rows)] = adjoint(strip, start, rows, upstream)
        return carry

    lax.fori_loop(0, length // rows, first, 0)
    for strip in range(strips):
        lanes = slice(strip * LANES, (strip + 1) * LANES)
        upstream = next_cot_ref[:, lanes].astype(jnp.float32)
        grad_pad[strip, length:] = adjoint(strip, length, HALO, upstream)

    def second(block, carry):
        start = pl.multiple_of(block * rows, rows)
        gate = jnp.broadcast_to(gate_ref[pl.ds(block, 1), :], (LANES, LANES)).T
        for strip in range(strips):
            lanes = slice(strip * LANES, (strip + 1) * LANES)
            total = cot_ref[pl.ds(start, rows), lanes].astype(jnp.float32)
            for tap in range(4):
                total = total + taps_ref[tap : tap + 1, lanes] * grad_pad[
                    strip, pl.ds(start + 3 * tap, rows)
                ]
            scaled[pl.ds(start, rows), lanes] = (gate * total).astype(jnp.bfloat16)
        return carry

    lax.fori_loop(0, length // rows, second, 0)
    place = 0
    own_width = heads * head_dim
    for low, high in pieces:
        for relative in range(tabs):
            base = ((tab_ref[0] + relative) % tabs) * own_width
            out = outs[place]
            place += 1
            for h in range(heads):
                start = pl.multiple_of(base + (h * head_dim + low), 16)
                term = lax.dot_general(
                    weight_ref[pl.ds(start, high - low), :],
                    scaled[...],
                    (((1,), (1,)), ((), ())),
                    preferred_element_type=jnp.float32,
                )
                out[h * (high - low) : (h + 1) * (high - low)] = term.astype(out.dtype)


def adjoint_terms(cot, value, prior, nexts, gate, taps, weight, pieces, heads, head_dim, tabs):
    length, width = cot.shape
    strips = width // LANES
    tab_index = lax.axis_index("tab").astype(jnp.int32).reshape(1)
    shapes = []
    for low, high in pieces:
        size = (heads * (high - low), length)
        shapes += [whole(size, jnp.float32)] + [whole(size, jnp.bfloat16)] * (tabs - 1)
    vmem = pl.BlockSpec(memory_space=pltpu.VMEM)
    return pl.pallas_call(
        lambda *refs: adjoint_kernel(
            *refs, pieces=pieces, heads=heads, head_dim=head_dim, tabs=tabs
        ),
        out_shape=shapes,
        in_specs=[pl.BlockSpec(memory_space=pltpu.SMEM)] + [vmem] * 8,
        out_specs=[vmem] * len(shapes),
        scratch_shapes=[
            pltpu.VMEM((strips, length + 2 * HALO, LANES), jnp.float32),
            pltpu.VMEM((strips, length + HALO, LANES), jnp.float32),
            pltpu.VMEM((length, width), jnp.bfloat16),
        ],
        name="adjoint",
    )(tab_index, cot, value, prior, nexts[0], nexts[1], gate, taps, weight)


def send_kernel(slot_ref, row_ref, own_ref, one_ref, two_ref, three_ref, out_ref, lhs, *, meta):
    heads, length = slot_ref.shape
    peers, tall, _ = out_ref.shape
    count = own_ref.shape[0] // heads
    cap = LANES // heads
    for h in range(heads):
        part = slice(h * count, (h + 1) * count)
        total = own_ref[part] + one_ref[part].astype(jnp.float32)
        total = total + two_ref[part].astype(jnp.float32) + three_ref[part].astype(jnp.float32)
        lhs[h, :count] = total.astype(jnp.bfloat16)
        if meta:
            number = row_ref[h : h + 1] + 1
            kind = lax.broadcasted_iota(jnp.int32, (2 * META, length), 0)
            digit = jnp.where(kind == 0, number // DIGIT, number % DIGIT)
            digit = jnp.where(kind == 2, 1, jnp.where(kind > 2, 0, digit))
            lhs[h, count:] = digit.astype(jnp.float32).astype(jnp.bfloat16)
    group = 4
    left = lax.broadcasted_iota(jnp.int32, (lhs.shape[1], LANES), 1) < cap
    place = lax.broadcasted_iota(jnp.int32, (group * cap, length), 0)

    def body(step, carry):
        base = step * (group * cap)
        sent = []
        for h in range(heads):
            chosen = jnp.where(slot_ref[h : h + 1] - base == place, 1.0, 0.0)
            sent.append(
                lax.dot_general(
                    lhs[h],
                    chosen.astype(jnp.bfloat16),
                    (((1,), (1,)), ((), ())),
                    preferred_element_type=jnp.float32,
                )
            )
        for pair in range(group // 2):
            a = sent[0][:, pair * LANES : (pair + 1) * LANES]
            b = sent[1][:, pair * LANES : (pair + 1) * LANES]
            even = jnp.where(left, a, pltpu.roll(b, cap, 1)).astype(jnp.bfloat16)
            odd = jnp.where(left, pltpu.roll(a, cap, 1), b).astype(jnp.bfloat16)
            out_ref[step * group + 2 * pair] = even[:tall]
            out_ref[step * group + 2 * pair + 1] = odd[:tall]
        return carry

    lax.fori_loop(0, peers // group, body, 0)


def send_blocks(slots, rows, terms, peers, meta):
    heads, length = slots.shape
    count = terms[0].shape[0] // heads
    tall = count + (META if meta else 0)
    padded = count + (2 * META if meta else 0)
    return pl.pallas_call(
        lambda *refs: send_kernel(*refs, meta=meta),
        out_shape=whole((peers, tall, LANES), jnp.bfloat16),
        scratch_shapes=[pltpu.VMEM((heads, padded, length), jnp.bfloat16)],
        name="send",
    )(slots, rows, *terms)


def update_kernel(got_ref, table_ref, one_ref, two_ref, new_table, new_one, new_two, grads):
    peers, tall, _ = got_ref.shape
    heads, rows, head_dim = table_ref.shape
    cap = LANES // heads
    left = lax.broadcasted_iota(jnp.int32, (tall, LANES), 1) < cap

    def spread(pair, carry):
        a = got_ref[2 * pair].astype(jnp.float32)
        b = got_ref[2 * pair + 1].astype(jnp.float32)
        lanes = pl.ds(pl.multiple_of(pair * LANES, LANES), LANES)
        grads[0, :, lanes] = jnp.where(left, a, pltpu.roll(b, cap, 1)).astype(jnp.bfloat16)
        grads[1, :, lanes] = jnp.where(left, pltpu.roll(a, cap, 1), b).astype(jnp.bfloat16)
        return carry

    lax.fori_loop(0, peers // 2, spread, 0)
    chunk = 512
    row_of = lax.broadcasted_iota(jnp.int32, (rows, chunk), 0)
    for h in range(heads):
        total = jnp.zeros((rows, tall), jnp.float32)
        for step in range(peers * cap // chunk):
            lanes = slice(step * chunk, (step + 1) * chunk)
            digits = grads[h, head_dim : head_dim + META, lanes].astype(jnp.float32)
            number = (digits[0:1] * float(DIGIT) + digits[1:2]).astype(jnp.int32) - 1
            chosen = jnp.where(number == row_of, 1.0, 0.0).astype(jnp.bfloat16)
            total = total + lax.dot_general(
                chosen, grads[h, :, lanes], (((1,), (1,)), ((), ())),
                preferred_element_type=jnp.float32,
            )
        touched = jnp.broadcast_to(total[:, head_dim + 2 : head_dim + 3] > 0.5, (rows, head_dim))
        grad = total[:, :head_dim]
        old_one, old_two, old_table = one_ref[h], two_ref[h], table_ref[h]
        first = beta_one * old_one + (1.0 - beta_one) * grad
        second = beta_two * old_two + (1.0 - beta_two) * grad * grad
        update = (first / (1.0 - beta_one**adam_steps)) / (
            jnp.sqrt(second / (1.0 - beta_two**adam_steps)) + epsilon
        )
        new_table[h] = jnp.where(touched, old_table - learn_rate * update, old_table)
        new_one[h] = jnp.where(touched, first, old_one)
        new_two[h] = jnp.where(touched, second, old_two)


def updated(got, table, one, two):
    peers, tall, _ = got.shape
    heads = table.shape[0]
    return pl.pallas_call(
        update_kernel,
        out_shape=[whole(table.shape, jnp.float32)] * 3,
        scratch_shapes=[pltpu.VMEM((heads, tall, peers * LANES // heads), jnp.bfloat16)],
        name="update",
    )(got, table, one, two)


def shards(
    cotangent,
    saved_value,
    gate_scale,
    conv_weight,
    value_weight,
    owner_ids,
    local_row,
    row_table,
    moment_one,
    moment_two,
):
    length = cotangent.shape[0]
    heads, _, head_dim = row_table.shape
    peers = lax.axis_size("seq")
    tabs = lax.axis_size("tab")
    cap = LANES // heads
    pieces = [(0, head_dim)]
    prior = shift_by(saved_value[length - HALO :], "seq", 1, False)
    nexts = [shift_by(x[:HALO], "seq", -1, False) for x in (saved_value, cotangent)]
    slots = slots_of(owner_ids[:, :, 0], peers, cap)
    terms = adjoint_terms(
        cotangent, saved_value, prior, nexts, gate_scale.reshape(-1, LANES), conv_weight,
        value_weight, pieces, heads, head_dim, tabs,
    )
    own, *others = terms
    parts = [own] + [shift_by(x, "tab", i + 1, True) for i, x in enumerate(others)]
    blocks = send_blocks(slots, local_row, parts, peers, True)
    got = lax.all_to_all(blocks, "seq", split_axis=0, concat_axis=0, tiled=True)
    return tuple(updated(got, row_table, moment_one, moment_two))


def solution(mesh):
    in_specs = (
        P("seq", "tab"),
        P("seq", "tab"),
        P("seq"),
        P(None, "tab"),
        P(None, "tab"),
        P("tab", "seq", None),
        P("tab", "seq"),
        P("tab", "seq", None),
        P("tab", "seq", None),
        P("tab", "seq", None),
    )
    out_specs = (P("tab", "seq", None), P("tab", "seq", None), P("tab", "seq", None))
    return jax.shard_map(shards, mesh=mesh, in_specs=in_specs, out_specs=out_specs, check_vma=False)
```

```python
import jax
import jax.numpy as jnp
from jax import lax
from jax.experimental import pallas as pl
from jax.experimental.pallas import tpu as pltpu
from jax.sharding import PartitionSpec as P


beta_one = 0.9
beta_two = 0.95
learn_rate = 0.01
adam_steps = 10.0
epsilon = 1e-08

LANES = 128
HALF = 64
HALO = 16
DIGIT = 32
META = 8
SMALL = 32
WIDE = 64
ROWS_DIMS = (((1,), (1,)), ((), ()))
VMEM = pl.BlockSpec(memory_space=pltpu.VMEM)
SMEM = pl.BlockSpec(memory_space=pltpu.SMEM)
ANY = pl.BlockSpec(memory_space=pl.ANY)


def shift_by(block, axis, distance, wrap):
    size = lax.axis_size(axis)
    if wrap:
        route = [(i, (i + distance) % size) for i in range(size)]
    else:
        route = [(i, i + distance) for i in range(size) if 0 <= i + distance < size]
    return lax.ppermute(block, axis, route)


def whole(shape, dtype):
    return jax.ShapeDtypeStruct(shape, dtype)


def near(*arrays):
    return [pltpu.with_memory_space_constraint(x, pltpu.VMEM) for x in arrays]


def lane_below(rows, bound):
    return lax.broadcasted_iota(jnp.int32, (rows, LANES), 1) < bound


def ones_where(mask):
    return jnp.where(mask, 1.0, 0.0).astype(jnp.bfloat16)


def plan_kernel(owners_ref, row_ref, place_ref, start_ref, meta_ref, rank_ref, *, peers):
    heads, length = owners_ref.shape
    owner_of = lax.broadcasted_iota(jnp.int32, (peers, LANES), 0)
    before = lax.broadcasted_iota(jnp.int32, (LANES, 2 * LANES), 0)
    after = lax.broadcasted_iota(jnp.int32, (LANES, 2 * LANES), 1)
    counter = ones_where((before < after) | (after >= LANES))
    carry = jnp.zeros((heads * peers, LANES), jnp.float32)
    for block in range(length // LANES):
        lanes = slice(block * LANES, (block + 1) * LANES)
        named = [
            jnp.where(owners_ref[h : h + 1, lanes] == owner_of, 1.0, 0.0) for h in range(heads)
        ]
        named = jnp.concatenate(named, axis=0)
        counts = jnp.dot(
            named.astype(jnp.bfloat16), counter, preferred_element_type=jnp.float32
        )
        rank = named * (counts[:, :LANES] + carry)
        carry = carry + counts[:, LANES:]
        for h in range(heads):
            own = jnp.sum(rank[h * peers : (h + 1) * peers], axis=0, keepdims=True)
            rank_ref[h : h + 1, lanes] = own
    owner_wide = lax.broadcasted_iota(jnp.int32, (LANES, length), 0)
    column = lax.broadcasted_iota(jnp.int32, (LANES, length), 0)
    total = jnp.zeros((2 * peers, LANES), jnp.float32)
    for h in range(heads):
        owners = owners_ref[h : h + 1]
        below = ones_where(owners < owner_wide)
        starts = lax.dot_general(
            jnp.ones((8, length), jnp.bfloat16), below, ROWS_DIMS,
            preferred_element_type=jnp.float32,
        )
        start_ref[h : h + 1] = starts[0:1].astype(jnp.int32)
        named = jnp.where(owners == owner_wide[:peers], 1.0, 0.0)
        start = jnp.sum(below[:peers].astype(jnp.float32), axis=1, keepdims=True)
        first = jnp.sum(named * start, axis=0, keepdims=True)
        rank = rank_ref[h : h + 1]
        place_ref[h : h + 1] = (first + rank).astype(jnp.int32)
        number = row_ref[h : h + 1] + 1
        high = (number // DIGIT).astype(jnp.float32)
        low = (number % DIGIT).astype(jnp.float32)
        digits = jnp.concatenate([named * high, named * low], axis=0).astype(jnp.bfloat16)
        chosen = ones_where(rank.astype(jnp.int32) + h * HALF == column)
        total = total + lax.dot_general(
            digits, chosen, ROWS_DIMS, preferred_element_type=jnp.float32
        )
    meta_ref[...] = total


def plan(owners, rows, peers):
    heads, length = owners.shape
    return pl.pallas_call(
        lambda *refs: plan_kernel(*refs, peers=peers),
        out_shape=[
            whole((heads, length), jnp.int32),
            whole((heads, LANES), jnp.int32),
            whole((2 * peers, LANES), jnp.float32),
        ],
        scratch_shapes=[pltpu.VMEM((heads, length), jnp.float32)],
        name="plan",
    )(owners, rows)


def weight_copies(tab_ref, weight_ref, packed, sems, spans, tabs, heads, head_dim):
    copies = []
    place = 0
    for relative in range(tabs):
        base = ((tab_ref[0] + relative) % tabs) * (heads * head_dim)
        for low, count in spans:
            for h in range(heads):
                start = pl.multiple_of(base + (h * head_dim + low), 32)
                copies.append(
                    pltpu.make_async_copy(
                        weight_ref.at[pl.ds(start, count)],
                        packed.at[pl.ds(place, count)],
                        sems.at[len(copies)],
                    )
                )
                place += count
    return copies


def adjoint_kernel(
    tab_ref, cot_ref, value_ref, prior_ref, next_ref, gate_ref, taps_ref, weight_ref,
    scaled, own_ref, one_ref, two_ref, three_ref, value_pad, grad_pad, packed, sems,
    *, heads, head_dim, tabs
):
    copies = weight_copies(
        tab_ref, weight_ref, packed, sems, [(0, SMALL)], tabs, heads, head_dim
    )
    for copy in copies:
        copy.start()
    length, width = cot_ref.shape
    strips = width // LANES
    rows = LANES
    for strip in range(strips):
        lanes = slice(strip * LANES, (strip + 1) * LANES)
        value_pad[strip, :HALO] = prior_ref[:, lanes].astype(jnp.float32)
        value_pad[strip, HALO : HALO + length] = value_ref[:, lanes].astype(jnp.float32)
        value_pad[strip, HALO + length :] = next_ref[:HALO, lanes].astype(jnp.float32)

    def adjoint(strip, start, count, upstream):
        lanes = slice(strip * LANES, (strip + 1) * LANES)
        mixed = taps_ref[0:1, lanes] * value_pad[strip, pl.ds(start + HALO, count)]
        for tap in range(1, 4):
            mixed = mixed + taps_ref[tap : tap + 1, lanes] * value_pad[
                strip, pl.ds(start + HALO - 3 * tap, count)
            ]
        squashed = jax.nn.sigmoid(mixed)
        return upstream * squashed * (1.0 + mixed * (1.0 - squashed))

    def first(block, carry):
        start = pl.multiple_of(block * rows, rows)
        for strip in range(strips):
            lanes = slice(strip * LANES, (strip + 1) * LANES)
            upstream = cot_ref[pl.ds(start, rows), lanes].astype(jnp.float32)
            grad_pad[strip, pl.ds(start, rows)] = adjoint(strip, start, rows, upstream)
        return carry

    lax.fori_loop(0, length // rows, first, 0)
    for strip in range(strips):
        lanes = slice(strip * LANES, (strip + 1) * LANES)
        upstream = next_ref[HALO:, lanes].astype(jnp.float32)
        grad_pad[strip, length:] = adjoint(strip, length, HALO, upstream)

    def second(block, carry):
        start = pl.multiple_of(block * rows, rows)
        gate = jnp.broadcast_to(gate_ref[pl.ds(block, 1), :], (LANES, LANES)).T
        for strip in range(strips):
            lanes = slice(strip * LANES, (strip + 1) * LANES)
            total = cot_ref[pl.ds(start, rows), lanes].astype(jnp.float32)
            for tap in range(4):
                total = total + taps_ref[tap : tap + 1, lanes] * grad_pad[
                    strip, pl.ds(start + 3 * tap, rows)
                ]
            scaled[pl.ds(start, rows), lanes] = (gate * total).astype(jnp.bfloat16)
        return carry

    lax.fori_loop(0, length // rows, second, 0)
    for copy in copies:
        copy.wait()
    fold = length // 2
    left = lane_below(fold, HALF)
    halves = [
        lax.dot_general(
            scaled[part * fold : (part + 1) * fold], packed[...], ROWS_DIMS,
            preferred_element_type=jnp.float32,
        )
        for part in range(2)
    ]
    outs = [own_ref, one_ref, two_ref, three_ref]
    for tile in range(2):
        lanes = slice(tile * LANES, (tile + 1) * LANES)
        a, b = halves[0][:, lanes], halves[1][:, lanes]
        even = jnp.where(left, a, pltpu.roll(b, HALF, 1))
        odd = jnp.where(left, pltpu.roll(a, HALF, 1), b)
        outs[2 * tile][...] = even.astype(outs[2 * tile].dtype)
        outs[2 * tile + 1][...] = odd.astype(outs[2 * tile + 1].dtype)


def adjoint_terms(tab_index, cot, value, prior, following, gate, taps, weight, heads, head_dim, tabs):
    length, width = cot.shape
    strips = width // LANES
    folded = (length // 2, LANES)
    return pl.pallas_call(
        lambda *refs: adjoint_kernel(*refs, heads=heads, head_dim=head_dim, tabs=tabs),
        out_shape=[whole((length, width), jnp.bfloat16), whole(folded, jnp.float32)]
        + [whole(folded, jnp.bfloat16)] * (tabs - 1),
        in_specs=[SMEM] + [VMEM] * 6 + [ANY],
        out_specs=[VMEM] * (tabs + 1),
        scratch_shapes=[
            pltpu.VMEM((strips, length + 2 * HALO, LANES), jnp.float32),
            pltpu.VMEM((strips, length + HALO, LANES), jnp.float32),
            pltpu.VMEM((tabs * heads * SMALL, width), jnp.bfloat16),
            pltpu.SemaphoreType.DMA((tabs * heads,)),
        ],
        name="adjoint",
    )(tab_index, cot, value, prior, following, gate, taps, weight)


def project_kernel(
    tab_ref, scaled_ref, weight_ref, own_ref, one_ref, two_ref, three_ref, packed, sems,
    *, heads, head_dim, tabs
):
    spans = [(SMALL, WIDE), (SMALL + WIDE, WIDE)]
    copies = weight_copies(tab_ref, weight_ref, packed, sems, spans, tabs, heads, head_dim)
    for copy in copies:
        copy.start()
    for copy in copies:
        copy.wait()
    size = 2 * LANES
    for relative, out in enumerate([own_ref, one_ref, two_ref, three_ref]):
        term = lax.dot_general(
            scaled_ref[...], packed[relative * size : (relative + 1) * size], ROWS_DIMS,
            preferred_element_type=jnp.float32,
        )
        out[...] = term.astype(out.dtype)


def project(tab_index, scaled, weight, heads, head_dim, tabs):
    length, width = scaled.shape
    size = (length, 2 * LANES)
    return pl.pallas_call(
        lambda *refs: project_kernel(*refs, heads=heads, head_dim=head_dim, tabs=tabs),
        out_shape=[whole(size, jnp.float32)] + [whole(size, jnp.bfloat16)] * (tabs - 1),
        in_specs=[SMEM, VMEM, ANY],
        out_specs=[VMEM] * tabs,
        scratch_shapes=[
            pltpu.VMEM((tabs * 2 * LANES, width), jnp.bfloat16),
            pltpu.SemaphoreType.DMA((tabs * heads * 2,)),
        ],
        name="project",
    )(tab_index, scaled, weight)


def sort_tokens(place_ref, grads, ordered, tiles):
    heads, length = place_ref.shape
    rows = 256
    position = lax.broadcasted_iota(jnp.int32, (rows, length), 0)
    for h in range(heads):
        for tile in range(tiles):
            ordered[h, tile, length:] = jnp.zeros((HALF, LANES), jnp.float32)
        for step in range(length // rows):
            chosen = ones_where(place_ref[h : h + 1] - step * rows == position)
            got = jnp.dot(chosen, grads[...], preferred_element_type=jnp.float32)
            for tile in range(tiles):
                ordered[h, tile, step * rows : (step + 1) * rows] = got[
                    :, tile * LANES : (tile + 1) * LANES
                ]


def summed(refs, index):
    total = refs[0][index]
    for ref in refs[1:]:
        total = total + ref[index].astype(jnp.float32)
    return total


def send_small_kernel(
    start_ref, place_ref, meta_ref, own_ref, one_ref, two_ref, three_ref, out_ref, grads, ordered
):
    peers = out_ref.shape[0]
    fold = own_ref.shape[0]
    wide_left = lane_below(fold, HALF)
    total = summed([own_ref, one_ref, two_ref, three_ref], slice(None))
    turned = pltpu.roll(total, HALF, 1)
    grads[:fold] = jnp.where(wide_left, total, turned).astype(jnp.bfloat16)
    grads[fold:] = jnp.where(wide_left, turned, total).astype(jnp.bfloat16)
    sort_tokens(place_ref, grads, ordered, 1)
    lane = lax.broadcasted_iota(jnp.int32, (SMALL, LANES), 1)
    kind = lax.broadcasted_iota(jnp.int32, (META, LANES), 0)
    unroll = 4

    def body(step, carry):
        for part in range(unroll):
            peer = step * unroll + part
            pieces = []
            for half in range(2):
                for h in range(2):
                    start = start_ref[h, peer] + half * SMALL
                    pieces.append(ordered[h, 0, pl.ds(start, SMALL)])
            block = jnp.where(lane < 32, pieces[0], pieces[1])
            upper = jnp.where(lane < 96, pieces[2], pieces[3])
            block = jnp.where(lane < 64, block, upper)
            out_ref[peer, :SMALL] = block.astype(jnp.bfloat16)
            high = jnp.broadcast_to(meta_ref[pl.ds(peer, 1)], (META, LANES))
            low = jnp.broadcast_to(meta_ref[pl.ds(peers + peer, 1)], (META, LANES))
            digits = jnp.where(kind == 0, high, jnp.where(kind == 1, low, 0.0))
            out_ref[peer, SMALL:] = digits.astype(jnp.bfloat16)
        return carry

    lax.fori_loop(0, peers // unroll, body, 0)


def send_small(starts, places, meta, terms, peers):
    heads, length = places.shape
    return pl.pallas_call(
        send_small_kernel,
        out_shape=whole((peers, SMALL + META, LANES), jnp.bfloat16),
        in_specs=[SMEM] + [VMEM] * 6,
        out_specs=VMEM,
        scratch_shapes=[
            pltpu.VMEM((length, LANES), jnp.bfloat16),
            pltpu.VMEM((heads, 1, length + HALF, LANES), jnp.float32),
        ],
        name="send_small",
    )(starts, places, meta, terms[0], *near(*terms[1:]))


def send_wide_kernel(
    start_ref, place_ref, own_ref, one_ref, two_ref, three_ref, after_ref, out_ref, grads, ordered
):
    peers = out_ref.shape[0]
    grads[...] = summed([own_ref, one_ref, two_ref, three_ref], slice(None)).astype(jnp.bfloat16)
    sort_tokens(place_ref, grads, ordered, 2)
    left = lane_below(HALF, HALF)
    unroll = 2

    def body(step, carry):
        for part in range(unroll):
            peer = step * unroll + part
            for tile in range(2):
                a = ordered[0, tile, pl.ds(start_ref[0, peer], HALF)]
                b = ordered[1, tile, pl.ds(start_ref[1, peer], HALF)]
                out_ref[peer, tile * HALF : (tile + 1) * HALF] = jnp.where(left, a, b).astype(
                    jnp.bfloat16
                )
        return carry

    lax.fori_loop(0, peers // unroll, body, 0)


def send_wide(starts, places, terms, after, peers):
    heads, length = places.shape
    return pl.pallas_call(
        send_wide_kernel,
        out_shape=whole((peers, 2 * HALF, LANES), jnp.bfloat16),
        in_specs=[SMEM] + [VMEM] * 5 + [ANY],
        out_specs=VMEM,
        scratch_shapes=[
            pltpu.VMEM((length, 2 * LANES), jnp.bfloat16),
            pltpu.VMEM((heads, 2, length + HALF, LANES), jnp.float32),
        ],
        name="send_wide",
    )(starts, places, terms[0], *near(*terms[1:]), after)


def add_small_kernel(got_ref, grad_ref, hits_ref, number_ref, numbers):
    peers = got_ref.shape[0]
    heads, _, rows = grad_ref.shape
    for peer in range(peers):
        digits = got_ref[peer, SMALL:].astype(jnp.float32)
        numbers[peer : peer + 1] = digits[0:1] * float(DIGIT) + digits[1:2] - 1.0
    pairs = peers // 2
    even = numbers[pl.ds(0, pairs, stride=2)]
    odd = numbers[pl.ds(1, pairs, stride=2)]
    left = lane_below(pairs, HALF)
    number_ref[0] = jnp.where(left, even, pltpu.roll(odd, HALF, 1)).astype(jnp.int32)
    number_ref[1] = jnp.where(left, pltpu.roll(even, HALF, 1), odd).astype(jnp.int32)
    row_of = lax.broadcasted_iota(jnp.int32, (rows, LANES), 0)
    keep = lane_below(SMALL, HALF)
    totals = [jnp.zeros((rows, LANES), jnp.float32) for _ in range(heads)]
    group = 4
    for step in range(peers // group):
        parts = []
        for peer in range(step * group, (step + 1) * group):
            block = got_ref[peer, :SMALL].astype(jnp.float32)
            parts.append(jnp.where(keep, block, 1.0))
            parts.append(jnp.where(keep, pltpu.roll(block, HALF, 1), 1.0))
        block = jnp.concatenate(parts, axis=0).astype(jnp.bfloat16)
        for h in range(heads):
            chosen = [
                ones_where(number_ref[h, 2 * step + i : 2 * step + i + 1] == row_of)
                for i in range(group // 2)
            ]
            totals[h] = totals[h] + jnp.dot(
                jnp.concatenate(chosen, axis=1), block, preferred_element_type=jnp.float32
            )
    for h in range(heads):
        turned = totals[h].T
        grad_ref[h] = turned[h * SMALL : (h + 1) * SMALL]
        hits_ref[h] = turned[HALF : HALF + 8]


def add_small(got, heads, rows):
    peers = got.shape[0]
    return pl.pallas_call(
        add_small_kernel,
        out_shape=[
            whole((heads, SMALL, rows), jnp.float32),
            whole((heads, 8, rows), jnp.float32),
            whole((heads, peers // 2, LANES), jnp.int32),
        ],
        scratch_shapes=[pltpu.VMEM((peers, LANES), jnp.float32)],
        name="add_small",
    )(*near(got))


def update_kernel(
    got_ref, small_ref, hits_ref, number_ref, table_ref, one_ref, two_ref,
    new_table, new_one, new_two
):
    peers = got_ref.shape[0]
    heads, head_dim, rows = table_ref.shape
    row_of = lax.broadcasted_iota(jnp.int32, (rows, LANES), 0)
    totals = [jnp.zeros((rows, 2 * LANES), jnp.float32) for _ in range(heads)]
    group = 4
    for step in range(peers // group):
        members = range(step * group, (step + 1) * group)
        block = jnp.concatenate(
            [
                jnp.concatenate([got_ref[peer, :HALF] for peer in members], axis=0),
                jnp.concatenate([got_ref[peer, HALF:] for peer in members], axis=0),
            ],
            axis=1,
        )
        for h in range(heads):
            chosen = [
                ones_where(number_ref[h, 2 * step + i : 2 * step + i + 1] == row_of)
                for i in range(group // 2)
            ]
            totals[h] = totals[h] + jnp.dot(
                jnp.concatenate(chosen, axis=1), block, preferred_element_type=jnp.float32
            )
    left = lane_below(rows, HALF)
    turned = [
        jnp.where(
            left, totals[0][:, t * LANES : (t + 1) * LANES], totals[1][:, t * LANES : (t + 1) * LANES]
        ).T
        for t in range(2)
    ]
    for h in range(heads):
        own = slice(h * HALF, (h + 1) * HALF)
        grad = jnp.concatenate([small_ref[h], turned[0][own], turned[1][own]], axis=0)
        touched = jnp.broadcast_to(hits_ref[h, 0:1] > 0.5, (head_dim, rows))
        old_one, old_two, old_table = one_ref[h], two_ref[h], table_ref[h]
        first = beta_one * old_one + (1.0 - beta_one) * grad
        second = beta_two * old_two + (1.0 - beta_two) * grad * grad
        update = (first / (1.0 - beta_one**adam_steps)) / (
            jnp.sqrt(second / (1.0 - beta_two**adam_steps)) + epsilon
        )
        new_table[h] = jnp.where(touched, old_table - learn_rate * update, old_table)
        new_one[h] = jnp.where(touched, first, old_one)
        new_two[h] = jnp.where(touched, second, old_two)


def updated(got, small, hits, numbers, table, one, two):
    return pl.pallas_call(
        update_kernel,
        out_shape=[whole(table.shape, jnp.float32)] * 3,
        name="update",
    )(*near(got), small, hits, numbers, table, one, two)


def shards(
    cotangent,
    saved_value,
    gate_scale,
    conv_weight,
    value_weight,
    owner_ids,
    local_row,
    row_table,
    moment_one,
    moment_two,
):
    length = cotangent.shape[0]
    heads, rows, head_dim = row_table.shape
    peers = lax.axis_size("seq")
    tabs = lax.axis_size("tab")
    tab_index = lax.axis_index("tab").astype(jnp.int32).reshape(1)
    prior = shift_by(saved_value[length - HALO :], "seq", 1, False)
    following = jnp.concatenate([saved_value[:HALO], cotangent[:HALO]], axis=0)
    following = shift_by(following, "seq", -1, False)
    places, starts, meta = plan(owner_ids[:, :, 0], local_row, peers)
    scaled, *small = adjoint_terms(
        tab_index, cotangent, saved_value, prior, following, gate_scale.reshape(-1, LANES),
        conv_weight, value_weight, heads, head_dim, tabs,
    )
    wide = list(project(tab_index, scaled, value_weight, heads, head_dim, tabs))
    for i in range(1, tabs):
        small[i] = shift_by(small[i], "tab", i, True)
        wide[i] = shift_by(wide[i], "tab", i, True)
    blocks = send_small(starts, places, meta, small, peers)
    got = lax.all_to_all(blocks, "seq", split_axis=0, concat_axis=0, tiled=True)
    wide_blocks = send_wide(starts, places, wide, blocks, peers)
    wide_got = lax.all_to_all(wide_blocks, "seq", split_axis=0, concat_axis=0, tiled=True)
    small_grad, hits, numbers = add_small(got, heads, rows)
    state = [jnp.swapaxes(x, 1, 2) for x in (row_table, moment_one, moment_two)]
    new = updated(wide_got, small_grad, hits, numbers, *state)
    return tuple(jnp.swapaxes(x, 1, 2) for x in new)


def solution(mesh):
    in_specs = (
        P("seq", "tab"),
        P("seq", "tab"),
        P("seq"),
        P(None, "tab"),
        P(None, "tab"),
        P("tab", "seq", None),
        P("tab", "seq"),
        P("tab", "seq", None),
        P("tab", "seq", None),
        P("tab", "seq", None),
    )
    out_specs = (P("tab", "seq", None), P("tab", "seq", None), P("tab", "seq", None))
    return jax.shard_map(shards, mesh=mesh, in_specs=in_specs, out_specs=out_specs, check_vma=False)
```

```python
import jax
import jax.numpy as jnp
from jax import lax
from jax.experimental import pallas as pl
from jax.experimental.pallas import tpu as pltpu
from jax.sharding import PartitionSpec as P


beta_one = 0.9
beta_two = 0.95
learn_rate = 0.01
adam_steps = 10.0
epsilon = 1e-08

LANES = 128
HALF = 64
HALO = 16
DIGIT = 32
META = 8
PIECES = 4
SMALL = 32
WIDE = 64
ROWS_DIMS = (((1,), (1,)), ((), ()))
VMEM = pl.BlockSpec(memory_space=pltpu.VMEM)
SMEM = pl.BlockSpec(memory_space=pltpu.SMEM)
ANY = pl.BlockSpec(memory_space=pl.ANY)
LIMIT = pltpu.CompilerParams(vmem_limit_bytes=24 << 20)


def shift_by(block, axis, distance, wrap):
    size = lax.axis_size(axis)
    if wrap:
        route = [(i, (i + distance) % size) for i in range(size)]
    else:
        route = [(i, i + distance) for i in range(size) if 0 <= i + distance < size]
    return lax.ppermute(block, axis, route)


def whole(shape, dtype):
    return jax.ShapeDtypeStruct(shape, dtype)


def kept(shape, dtype):
    return pltpu.VMEM(shape, dtype)


def near(*arrays):
    return [pltpu.with_memory_space_constraint(x, pltpu.VMEM) for x in arrays]


def far(*arrays):
    return [pltpu.with_memory_space_constraint(x, pltpu.HBM) for x in arrays]


def lane_below(rows, bound):
    return lax.broadcasted_iota(jnp.int32, (rows, LANES), 1) < bound


def ones_where(mask):
    return jnp.where(mask, 1.0, 0.0).astype(jnp.bfloat16)


def plan_kernel(owners_ref, row_ref, place_ref, start_ref, meta_ref, rank_ref, *, peers):
    heads, _, length = owners_ref.shape
    owner_of = lax.broadcasted_iota(jnp.int32, (peers, LANES), 0)
    before = lax.broadcasted_iota(jnp.int32, (LANES, 2 * LANES), 0)
    after = lax.broadcasted_iota(jnp.int32, (LANES, 2 * LANES), 1)
    counter = ones_where((before < after) | (after >= LANES))
    carry = jnp.zeros((heads * peers, LANES), jnp.float32)
    for block in range(length // LANES):
        lanes = slice(block * LANES, (block + 1) * LANES)
        named = [
            jnp.where(owners_ref[h, :, lanes] == owner_of, 1.0, 0.0) for h in range(heads)
        ]
        named = jnp.concatenate(named, axis=0)
        counts = jnp.dot(
            named.astype(jnp.bfloat16), counter, preferred_element_type=jnp.float32
        )
        rank = named * (counts[:, :LANES] + carry)
        carry = carry + counts[:, LANES:]
        for h in range(heads):
            own = jnp.sum(rank[h * peers : (h + 1) * peers], axis=0, keepdims=True)
            rank_ref[h : h + 1, lanes] = own
    owner_wide = lax.broadcasted_iota(jnp.int32, (LANES, length), 0)
    column = lax.broadcasted_iota(jnp.int32, (LANES, length), 0)
    total = jnp.zeros((2 * peers, LANES), jnp.float32)
    for h in range(heads):
        owners = owners_ref[h]
        below = ones_where(owners < owner_wide)
        starts = lax.dot_general(
            jnp.ones((8, length), jnp.bfloat16), below, ROWS_DIMS,
            preferred_element_type=jnp.float32,
        )
        start_ref[h : h + 1] = starts[0:1].astype(jnp.int32)
        named = jnp.where(owners == owner_wide[:peers], 1.0, 0.0)
        start = jnp.sum(below[:peers].astype(jnp.float32), axis=1, keepdims=True)
        first = jnp.sum(named * start, axis=0, keepdims=True)
        rank = rank_ref[h : h + 1]
        place_ref[h : h + 1] = (first + rank).astype(jnp.int32)
        number = row_ref[h : h + 1] + 1
        high = (number // DIGIT).astype(jnp.float32)
        low = (number % DIGIT).astype(jnp.float32)
        digits = jnp.concatenate([named * high, named * low], axis=0).astype(jnp.bfloat16)
        chosen = ones_where(rank.astype(jnp.int32) + h * HALF == column)
        total = total + lax.dot_general(
            digits, chosen, ROWS_DIMS, preferred_element_type=jnp.float32
        )
    meta_ref[...] = total


def plan(owners, rows, peers):
    heads, _, length = owners.shape
    return pl.pallas_call(
        lambda *refs: plan_kernel(*refs, peers=peers),
        out_shape=[
            whole((heads, length), jnp.int32),
            whole((heads, LANES), jnp.int32),
            whole((2 * peers, LANES), jnp.float32),
        ],
        scratch_shapes=[pltpu.VMEM((heads, length), jnp.float32)],
        compiler_params=LIMIT,
        name="plan",
    )(*far(owners, rows))


def weight_copies(
    tab_ref, weight_ref, packed, sems, spans, tabs, heads, head_dim, relatives=None
):
    copies = []
    place = 0
    for relative in range(tabs) if relatives is None else relatives:
        base = ((tab_ref[0] + relative) % tabs) * (heads * head_dim)
        for low, count in spans:
            for h in range(heads):
                start = pl.multiple_of(base + (h * head_dim + low), 32)
                copies.append(
                    pltpu.make_async_copy(
                        weight_ref.at[pl.ds(start, count)],
                        packed.at[pl.ds(place, count)],
                        sems.at[len(copies)],
                    )
                )
                place += count
    return copies


def adjoint_kernel(
    tab_ref, cot_far, value_far, prior_ref, next_ref, gate_ref, taps_ref, weight_ref, after_ref,
    scaled, own_ref, one_ref, two_ref, three_ref,
    cot_ref, value_ref, value_pad, grad_pad, packed, sems, cot_sems, value_sems,
    *, heads, head_dim, tabs
):
    length, width = cot_ref.shape
    piece = length // PIECES
    loads = []
    for index in range(PIECES):
        part = pl.ds(index * piece, piece)
        for source, target, own in (
            (value_far, value_ref, value_sems), (cot_far, cot_ref, cot_sems)
        ):
            loads.append(pltpu.make_async_copy(source.at[part], target.at[part], own.at[index]))
            loads[-1].start()
    copies = weight_copies(
        tab_ref, weight_ref, packed, sems, [(0, SMALL)], tabs, heads, head_dim
    )
    for copy in copies:
        copy.start()
    strips = width // LANES
    rows = LANES
    for strip in range(strips):
        lanes = slice(strip * LANES, (strip + 1) * LANES)
        value_pad[strip, :HALO] = prior_ref[:, lanes].astype(jnp.float32)
        value_pad[strip, HALO + length :] = next_ref[:HALO, lanes].astype(jnp.float32)

    def adjoint(strip, start, count, upstream):
        lanes = slice(strip * LANES, (strip + 1) * LANES)
        mixed = taps_ref[0:1, lanes] * value_pad[strip, pl.ds(start + HALO, count)]
        for tap in range(1, 4):
            mixed = mixed + taps_ref[tap : tap + 1, lanes] * value_pad[
                strip, pl.ds(start + HALO - 3 * tap, count)
            ]
        squashed = jax.nn.sigmoid(mixed)
        return upstream * squashed * (1.0 + mixed * (1.0 - squashed))

    def first(block, carry):
        start = pl.multiple_of(block * rows, rows)
        for strip in range(strips):
            lanes = slice(strip * LANES, (strip + 1) * LANES)
            value_pad[strip, pl.ds(start + HALO, rows)] = value_ref[
                pl.ds(start, rows), lanes
            ].astype(jnp.float32)
            upstream = cot_ref[pl.ds(start, rows), lanes].astype(jnp.float32)
            grad_pad[strip, pl.ds(start, rows)] = adjoint(strip, start, rows, upstream)
        return carry

    for index in range(PIECES):
        loads[2 * index].wait()
        loads[2 * index + 1].wait()
        lax.fori_loop(index * (piece // rows), (index + 1) * (piece // rows), first, 0)
    for strip in range(strips):
        lanes = slice(strip * LANES, (strip + 1) * LANES)
        upstream = next_ref[HALO:, lanes].astype(jnp.float32)
        grad_pad[strip, length:] = adjoint(strip, length, HALO, upstream)

    def second(block, carry):
        start = pl.multiple_of(block * rows, rows)
        gate = jnp.broadcast_to(gate_ref[pl.ds(block, 1), :], (LANES, LANES)).T
        for strip in range(strips):
            lanes = slice(strip * LANES, (strip + 1) * LANES)
            total = cot_ref[pl.ds(start, rows), lanes].astype(jnp.float32)
            for tap in range(4):
                total = total + taps_ref[tap : tap + 1, lanes] * grad_pad[
                    strip, pl.ds(start + 3 * tap, rows)
                ]
            scaled[pl.ds(start, rows), lanes] = (gate * total).astype(jnp.bfloat16)
        return carry

    lax.fori_loop(0, length // rows, second, 0)
    for copy in copies:
        copy.wait()
    fold = length // 2
    left = lane_below(fold, HALF)
    halves = [
        lax.dot_general(
            scaled[part * fold : (part + 1) * fold], packed[...], ROWS_DIMS,
            preferred_element_type=jnp.float32,
        )
        for part in range(2)
    ]
    outs = [own_ref, one_ref, two_ref, three_ref]
    for tile in range(2):
        lanes = slice(tile * LANES, (tile + 1) * LANES)
        a, b = halves[0][:, lanes], halves[1][:, lanes]
        even = jnp.where(left, a, pltpu.roll(b, HALF, 1))
        odd = jnp.where(left, pltpu.roll(a, HALF, 1), b)
        outs[2 * tile][...] = even.astype(outs[2 * tile].dtype)
        outs[2 * tile + 1][...] = odd.astype(outs[2 * tile + 1].dtype)


def adjoint_terms(
    tab_index, cot, value, prior, following, gate, taps, weight, after, heads, head_dim, tabs
):
    length, width = cot.shape
    strips = width // LANES
    folded = (length // 2, LANES)
    return pl.pallas_call(
        lambda *refs: adjoint_kernel(*refs, heads=heads, head_dim=head_dim, tabs=tabs),
        out_shape=[kept((length, width), jnp.bfloat16), kept(folded, jnp.float32)]
        + [kept(folded, jnp.bfloat16)] * (tabs - 1),
        in_specs=[SMEM] + [ANY] * 2 + [VMEM] * 4 + [ANY] * 2,
        out_specs=[VMEM] * (tabs + 1),
        scratch_shapes=[
            pltpu.VMEM((length, width), jnp.bfloat16),
            pltpu.VMEM((length, width), jnp.bfloat16),
            pltpu.VMEM((strips, length + 2 * HALO, LANES), jnp.float32),
            pltpu.VMEM((strips, length + HALO, LANES), jnp.float32),
            pltpu.VMEM((tabs * heads * SMALL, width), jnp.bfloat16),
            pltpu.SemaphoreType.DMA((tabs * heads,)),
            pltpu.SemaphoreType.DMA((PIECES,)),
            pltpu.SemaphoreType.DMA((PIECES,)),
        ],
        compiler_params=LIMIT,
        name="adjoint",
    )(tab_index, *far(cot, value), *near(prior, following), *far(gate, taps, weight), after)


def project_kernel(
    tab_ref, scaled_ref, weight_ref, after_ref, *refs, heads, head_dim, tabs, relatives
):
    *outs, packed, sems = refs
    spans = [(SMALL, WIDE), (SMALL + WIDE, WIDE)]
    copies = weight_copies(
        tab_ref, weight_ref, packed, sems, spans, tabs, heads, head_dim, relatives
    )
    for copy in copies:
        copy.start()
    size = 2 * LANES
    each = len(copies) // len(outs)
    for index, out in enumerate(outs):
        for copy in copies[index * each : (index + 1) * each]:
            copy.wait()
        term = lax.dot_general(
            scaled_ref[...], packed[index * size : (index + 1) * size], ROWS_DIMS,
            preferred_element_type=jnp.float32,
        )
        out[...] = term.astype(out.dtype)


def project(tab_index, scaled, weight, after, heads, head_dim, tabs, relatives, dtype):
    length, width = scaled.shape
    size = (length, 2 * LANES)
    count = len(relatives)
    return pl.pallas_call(
        lambda *refs: project_kernel(
            *refs, heads=heads, head_dim=head_dim, tabs=tabs, relatives=relatives
        ),
        out_shape=[kept(size, dtype)] * count,
        in_specs=[SMEM, VMEM, ANY, ANY],
        out_specs=[VMEM] * count,
        scratch_shapes=[
            pltpu.VMEM((count * 2 * LANES, width), jnp.bfloat16),
            pltpu.SemaphoreType.DMA((count * heads * 2,)),
        ],
        compiler_params=LIMIT,
        name="project",
    )(tab_index, *near(scaled), *far(weight), after)


def sort_tokens(place_ref, grads, ordered, tiles):
    heads, length = place_ref.shape
    rows = 256
    position = lax.broadcasted_iota(jnp.int32, (rows, length), 0)
    for h in range(heads):
        for tile in range(tiles):
            ordered[h, tile, length:] = jnp.zeros((HALF, LANES), jnp.float32)
        for step in range(length // rows):
            chosen = ones_where(place_ref[h : h + 1] - step * rows == position)
            got = jnp.dot(chosen, grads[...], preferred_element_type=jnp.float32)
            for tile in range(tiles):
                ordered[h, tile, step * rows : (step + 1) * rows] = got[
                    :, tile * LANES : (tile + 1) * LANES
                ]


def summed(refs, index):
    total = refs[0][index]
    for ref in refs[1:]:
        total = total + ref[index].astype(jnp.float32)
    return total


def send_small_kernel(
    start_ref, place_ref, meta_ref, own_ref, one_ref, two_ref, three_ref, out_ref, grads, ordered
):
    peers = out_ref.shape[0]
    fold = own_ref.shape[0]
    wide_left = lane_below(fold, HALF)
    total = summed([own_ref, one_ref, two_ref, three_ref], slice(None))
    turned = pltpu.roll(total, HALF, 1)
    grads[:fold] = jnp.where(wide_left, total, turned).astype(jnp.bfloat16)
    grads[fold:] = jnp.where(wide_left, turned, total).astype(jnp.bfloat16)
    sort_tokens(place_ref, grads, ordered, 1)
    lane = lax.broadcasted_iota(jnp.int32, (SMALL, LANES), 1)
    kind = lax.broadcasted_iota(jnp.int32, (META, LANES), 0)
    unroll = 4

    def body(step, carry):
        for part in range(unroll):
            peer = step * unroll + part
            pieces = []
            for half in range(2):
                for h in range(2):
                    start = start_ref[h, peer] + half * SMALL
                    pieces.append(ordered[h, 0, pl.ds(start, SMALL)])
            block = jnp.where(lane < 32, pieces[0], pieces[1])
            upper = jnp.where(lane < 96, pieces[2], pieces[3])
            block = jnp.where(lane < 64, block, upper)
            out_ref[peer, :SMALL] = block.astype(jnp.bfloat16)
            high = jnp.broadcast_to(meta_ref[pl.ds(peer, 1)], (META, LANES))
            low = jnp.broadcast_to(meta_ref[pl.ds(peers + peer, 1)], (META, LANES))
            digits = jnp.where(kind == 0, high, jnp.where(kind == 1, low, 0.0))
            out_ref[peer, SMALL:] = digits.astype(jnp.bfloat16)
        return carry

    lax.fori_loop(0, peers // unroll, body, 0)


def send_small(starts, places, meta, terms, peers):
    heads, length = places.shape
    return pl.pallas_call(
        send_small_kernel,
        out_shape=kept((peers, SMALL + META, LANES), jnp.bfloat16),
        in_specs=[SMEM] + [VMEM] * 6,
        out_specs=VMEM,
        scratch_shapes=[
            pltpu.VMEM((length, LANES), jnp.bfloat16),
            pltpu.VMEM((heads, 1, length + HALF, LANES), jnp.float32),
        ],
        compiler_params=LIMIT,
        name="send_small",
    )(starts, places, meta, *near(*terms))


def send_wide_kernel(
    start_ref, place_ref, own_ref, one_ref, two_ref, three_ref, after_ref, out_ref, grads, ordered
):
    peers = out_ref.shape[0]
    grads[...] = summed([own_ref, one_ref, two_ref, three_ref], slice(None)).astype(jnp.bfloat16)
    sort_tokens(place_ref, grads, ordered, 2)
    left = lane_below(HALF, HALF)
    unroll = 2

    def body(step, carry):
        for part in range(unroll):
            peer = step * unroll + part
            for tile in range(2):
                a = ordered[0, tile, pl.ds(start_ref[0, peer], HALF)]
                b = ordered[1, tile, pl.ds(start_ref[1, peer], HALF)]
                out_ref[peer, tile * HALF : (tile + 1) * HALF] = jnp.where(left, a, b).astype(
                    jnp.bfloat16
                )
        return carry

    lax.fori_loop(0, peers // unroll, body, 0)


def send_wide(starts, places, terms, after, peers):
    heads, length = places.shape
    return pl.pallas_call(
        send_wide_kernel,
        out_shape=kept((peers, 2 * HALF, LANES), jnp.bfloat16),
        in_specs=[SMEM] + [VMEM] * 5 + [ANY],
        out_specs=VMEM,
        scratch_shapes=[
            pltpu.VMEM((length, 2 * LANES), jnp.bfloat16),
            pltpu.VMEM((heads, 2, length + HALF, LANES), jnp.float32),
        ],
        compiler_params=LIMIT,
        name="send_wide",
    )(starts, places, *near(*terms), after)


def add_small_kernel(got_ref, grad_ref, hits_ref, number_ref, numbers):
    peers = got_ref.shape[0]
    heads, _, rows = grad_ref.shape
    for peer in range(peers):
        digits = got_ref[peer, SMALL:].astype(jnp.float32)
        numbers[peer : peer + 1] = digits[0:1] * float(DIGIT) + digits[1:2] - 1.0
    pairs = peers // 2
    even = numbers[pl.ds(0, pairs, stride=2)]
    odd = numbers[pl.ds(1, pairs, stride=2)]
    left = lane_below(pairs, HALF)
    number_ref[0] = jnp.where(left, even, pltpu.roll(odd, HALF, 1)).astype(jnp.int32)
    number_ref[1] = jnp.where(left, pltpu.roll(even, HALF, 1), odd).astype(jnp.int32)
    row_of = lax.broadcasted_iota(jnp.int32, (rows, LANES), 0)
    keep = lane_below(SMALL, HALF)
    totals = [jnp.zeros((rows, LANES), jnp.float32) for _ in range(heads)]
    group = 4
    for step in range(peers // group):
        parts = []
        for peer in range(step * group, (step + 1) * group):
            block = got_ref[peer, :SMALL].astype(jnp.float32)
            parts.append(jnp.where(keep, block, 1.0))
            parts.append(jnp.where(keep, pltpu.roll(block, HALF, 1), 1.0))
        block = jnp.concatenate(parts, axis=0).astype(jnp.bfloat16)
        for h in range(heads):
            chosen = [
                ones_where(number_ref[h, 2 * step + i : 2 * step + i + 1] == row_of)
                for i in range(group // 2)
            ]
            totals[h] = totals[h] + jnp.dot(
                jnp.concatenate(chosen, axis=1), block, preferred_element_type=jnp.float32
            )
    for h in range(heads):
        turned = totals[h].T
        grad_ref[h] = turned[h * SMALL : (h + 1) * SMALL]
        hits_ref[h] = turned[HALF : HALF + 8]


def add_small(got, heads, rows):
    peers = got.shape[0]
    return pl.pallas_call(
        add_small_kernel,
        out_shape=[
            kept((heads, SMALL, rows), jnp.float32),
            kept((heads, 8, rows), jnp.float32),
            kept((heads, peers // 2, LANES), jnp.int32),
        ],
        scratch_shapes=[pltpu.VMEM((peers, LANES), jnp.float32)],
        compiler_params=LIMIT,
        name="add_small",
    )(*near(got))


def update_kernel(
    got_ref, small_ref, hits_ref, number_ref, table_far, one_far, two_far,
    new_table, new_one, new_two, table_ref, one_ref, two_ref, sems
):
    loads = [
        pltpu.make_async_copy(source, target, sems.at[index])
        for index, (source, target) in enumerate(
            [(table_far, table_ref), (one_far, one_ref), (two_far, two_ref)]
        )
    ]
    for load in loads:
        load.start()
    peers = got_ref.shape[0]
    heads, head_dim, rows = table_ref.shape
    row_of = lax.broadcasted_iota(jnp.int32, (rows, LANES), 0)
    totals = [jnp.zeros((rows, 2 * LANES), jnp.float32) for _ in range(heads)]
    group = 4
    for step in range(peers // group):
        members = range(step * group, (step + 1) * group)
        block = jnp.concatenate(
            [
                jnp.concatenate([got_ref[peer, :HALF] for peer in members], axis=0),
                jnp.concatenate([got_ref[peer, HALF:] for peer in members], axis=0),
            ],
            axis=1,
        )
        for h in range(heads):
            chosen = [
                ones_where(number_ref[h, 2 * step + i : 2 * step + i + 1] == row_of)
                for i in range(group // 2)
            ]
            totals[h] = totals[h] + jnp.dot(
                jnp.concatenate(chosen, axis=1), block, preferred_element_type=jnp.float32
            )
    for load in loads:
        load.wait()
    left = lane_below(rows, HALF)
    turned = [
        jnp.where(
            left, totals[0][:, t * LANES : (t + 1) * LANES], totals[1][:, t * LANES : (t + 1) * LANES]
        ).T
        for t in range(2)
    ]
    for h in range(heads):
        own = slice(h * HALF, (h + 1) * HALF)
        grad = jnp.concatenate([small_ref[h], turned[0][own], turned[1][own]], axis=0)
        touched = jnp.broadcast_to(hits_ref[h, 0:1] > 0.5, (head_dim, rows))
        old_one, old_two, old_table = one_ref[h], two_ref[h], table_ref[h]
        first = beta_one * old_one + (1.0 - beta_one) * grad
        second = beta_two * old_two + (1.0 - beta_two) * grad * grad
        update = (first / (1.0 - beta_one**adam_steps)) / (
            jnp.sqrt(second / (1.0 - beta_two**adam_steps)) + epsilon
        )
        new_table[h] = jnp.where(touched, old_table - learn_rate * update, old_table)
        new_one[h] = jnp.where(touched, first, old_one)
        new_two[h] = jnp.where(touched, second, old_two)


def updated(got, small, hits, numbers, table, one, two):
    return pl.pallas_call(
        update_kernel,
        out_shape=[whole(table.shape, jnp.float32)] * 3,
        in_specs=[VMEM] * 4 + [ANY] * 3,
        out_specs=[VMEM] * 3,
        scratch_shapes=[pltpu.VMEM(table.shape, jnp.float32)] * 3
        + [pltpu.SemaphoreType.DMA((3,))],
        compiler_params=LIMIT,
        name="update",
    )(*near(got, small, hits, numbers), *far(table, one, two))


def shards(
    cotangent,
    saved_value,
    gate_scale,
    conv_weight,
    value_weight,
    owner_ids,
    local_row,
    row_table,
    moment_one,
    moment_two,
):
    length = cotangent.shape[0]
    heads, rows, head_dim = row_table.shape
    peers = lax.axis_size("seq")
    tabs = lax.axis_size("tab")
    tab_index = lax.axis_index("tab").astype(jnp.int32).reshape(1)
    prior = shift_by(saved_value[length - HALO :], "seq", 1, False)
    following = jnp.concatenate([saved_value[:HALO], cotangent[:HALO]], axis=0)
    following = shift_by(following, "seq", -1, False)
    places, starts, meta = plan(jnp.swapaxes(owner_ids, 1, 2), local_row, peers)
    scaled, *small = adjoint_terms(
        tab_index, cotangent, saved_value, prior, following, gate_scale.reshape(-1, LANES),
        conv_weight, value_weight, places, heads, head_dim, tabs,
    )
    sizes = (heads, head_dim, tabs)
    wide = [None] + list(
        project(
            tab_index, scaled, value_weight, tab_index, *sizes, range(1, tabs), jnp.bfloat16
        )
    )
    for i in range(1, tabs):
        small[i] = shift_by(small[i], "tab", i, True)
        wide[i] = shift_by(wide[i], "tab", i, True)
    blocks = send_small(starts, places, meta, small, peers)
    got = lax.all_to_all(blocks, "seq", split_axis=0, concat_axis=0, tiled=True)
    wide[:1] = project(
        tab_index, scaled, value_weight, blocks, *sizes, range(1), jnp.float32
    )
    wide_blocks = send_wide(starts, places, wide, blocks, peers)
    wide_got = lax.all_to_all(wide_blocks, "seq", split_axis=0, concat_axis=0, tiled=True)
    small_grad, hits, numbers = add_small(got, heads, rows)
    state = [jnp.swapaxes(x, 1, 2) for x in (row_table, moment_one, moment_two)]
    new = updated(wide_got, small_grad, hits, numbers, *state)
    return tuple(jnp.swapaxes(x, 1, 2) for x in new)


def solution(mesh):
    in_specs = (
        P("seq", "tab"),
        P("seq", "tab"),
        P("seq"),
        P(None, "tab"),
        P(None, "tab"),
        P("tab", "seq", None),
        P("tab", "seq"),
        P("tab", "seq", None),
        P("tab", "seq", None),
        P("tab", "seq", None),
    )
    out_specs = (P("tab", "seq", None), P("tab", "seq", None), P("tab", "seq", None))
    return jax.shard_map(shards, mesh=mesh, in_specs=in_specs, out_specs=out_specs, check_vma=False)
```

```python
import jax
import jax.numpy as jnp
from jax import lax
from jax.experimental import pallas as pl
from jax.experimental.pallas import tpu as pltpu
from jax.sharding import PartitionSpec as P


beta_one = 0.9
beta_two = 0.95
learn_rate = 0.01
adam_steps = 10.0
epsilon = 1e-08

LANES = 128
HALF = 64
HALO = 16
DIGIT = 32
META = 8
PIECES = 4
SMALL = 32
WIDE = 64
ROWS_DIMS = (((1,), (1,)), ((), ()))
VMEM = pl.BlockSpec(memory_space=pltpu.VMEM)
SMEM = pl.BlockSpec(memory_space=pltpu.SMEM)
ANY = pl.BlockSpec(memory_space=pl.ANY)
LIMIT = pltpu.CompilerParams(vmem_limit_bytes=24 << 20)


def shift_by(block, axis, distance, wrap):
    size = lax.axis_size(axis)
    if wrap:
        route = [(i, (i + distance) % size) for i in range(size)]
    else:
        route = [(i, i + distance) for i in range(size) if 0 <= i + distance < size]
    return lax.ppermute(block, axis, route)


def whole(shape, dtype):
    return jax.ShapeDtypeStruct(shape, dtype)


def kept(shape, dtype):
    return pltpu.VMEM(shape, dtype)


def near(*arrays):
    return [pltpu.with_memory_space_constraint(x, pltpu.VMEM) for x in arrays]


def far(*arrays):
    return [pltpu.with_memory_space_constraint(x, pltpu.HBM) for x in arrays]


def lane_below(rows, bound):
    return lax.broadcasted_iota(jnp.int32, (rows, LANES), 1) < bound


def ones_where(mask):
    return jnp.where(mask, 1.0, 0.0).astype(jnp.bfloat16)


def plan_kernel(owners_ref, row_ref, place_ref, start_ref, meta_ref, rank_ref, *, peers):
    heads, _, length = owners_ref.shape
    owner_of = lax.broadcasted_iota(jnp.int32, (peers, LANES), 0)
    before = lax.broadcasted_iota(jnp.int32, (LANES, 2 * LANES), 0)
    after = lax.broadcasted_iota(jnp.int32, (LANES, 2 * LANES), 1)
    counter = ones_where((before < after) | (after >= LANES))
    carry = jnp.zeros((heads * peers, LANES), jnp.float32)
    for block in range(length // LANES):
        lanes = slice(block * LANES, (block + 1) * LANES)
        named = [
            jnp.where(owners_ref[h, :, lanes] == owner_of, 1.0, 0.0) for h in range(heads)
        ]
        named = jnp.concatenate(named, axis=0)
        counts = jnp.dot(
            named.astype(jnp.bfloat16), counter, preferred_element_type=jnp.float32
        )
        rank = named * (counts[:, :LANES] + carry)
        carry = carry + counts[:, LANES:]
        for h in range(heads):
            own = jnp.sum(rank[h * peers : (h + 1) * peers], axis=0, keepdims=True)
            rank_ref[h : h + 1, lanes] = own
    owner_wide = lax.broadcasted_iota(jnp.int32, (LANES, length), 0)
    column = lax.broadcasted_iota(jnp.int32, (LANES, length), 0)
    total = jnp.zeros((2 * peers, LANES), jnp.float32)
    for h in range(heads):
        owners = owners_ref[h]
        below = ones_where(owners < owner_wide)
        starts = lax.dot_general(
            jnp.ones((8, length), jnp.bfloat16), below, ROWS_DIMS,
            preferred_element_type=jnp.float32,
        )
        start_ref[h : h + 1] = starts[0:1].astype(jnp.int32)
        named = jnp.where(owners == owner_wide[:peers], 1.0, 0.0)
        start = jnp.sum(below[:peers].astype(jnp.float32), axis=1, keepdims=True)
        first = jnp.sum(named * start, axis=0, keepdims=True)
        rank = rank_ref[h : h + 1]
        place_ref[h : h + 1] = (first + rank).astype(jnp.int32)
        number = row_ref[h : h + 1] + 1
        high = (number // DIGIT).astype(jnp.float32)
        low = (number % DIGIT).astype(jnp.float32)
        digits = jnp.concatenate([named * high, named * low], axis=0).astype(jnp.bfloat16)
        chosen = ones_where(rank.astype(jnp.int32) + h * HALF == column)
        total = total + lax.dot_general(
            digits, chosen, ROWS_DIMS, preferred_element_type=jnp.float32
        )
    meta_ref[...] = total


def plan(owners, rows, peers):
    heads, _, length = owners.shape
    return pl.pallas_call(
        lambda *refs: plan_kernel(*refs, peers=peers),
        out_shape=[
            whole((heads, length), jnp.int32),
            whole((heads, LANES), jnp.int32),
            whole((2 * peers, LANES), jnp.float32),
        ],
        scratch_shapes=[pltpu.VMEM((heads, length), jnp.float32)],
        compiler_params=LIMIT,
        name="plan",
    )(*far(owners, rows))


def weight_copies(
    tab_ref, weight_ref, packed, sems, spans, tabs, heads, head_dim, relatives=None
):
    copies = []
    place = 0
    for relative in range(tabs) if relatives is None else relatives:
        base = ((tab_ref[0] + relative) % tabs) * (heads * head_dim)
        for low, count in spans:
            for h in range(heads):
                start = pl.multiple_of(base + (h * head_dim + low), 32)
                copies.append(
                    pltpu.make_async_copy(
                        weight_ref.at[pl.ds(start, count)],
                        packed.at[pl.ds(place, count)],
                        sems.at[len(copies)],
                    )
                )
                place += count
    return copies


def edges_kernel(value_far, cot_far, prior_ref, next_ref, value_ref, cot_ref, sems):
    length = value_far.shape[0]
    head, tail = pl.ds(0, HALO), pl.ds(length - HALO, HALO)
    wide_head, wide_tail = pl.ds(0, 2 * HALO), pl.ds(length - 2 * HALO, 2 * HALO)
    moves = [
        (value_far.at[tail], prior_ref),
        (value_far.at[head], next_ref.at[pl.ds(0, HALO)]),
        (cot_far.at[head], next_ref.at[pl.ds(HALO, HALO)]),
        (value_far.at[wide_head], value_ref.at[pl.ds(0, 2 * HALO)]),
        (value_far.at[wide_tail], value_ref.at[pl.ds(2 * HALO, 2 * HALO)]),
        (cot_far.at[wide_head], cot_ref.at[pl.ds(0, 2 * HALO)]),
        (cot_far.at[tail], cot_ref.at[pl.ds(2 * HALO, HALO)]),
    ]
    copies = [pltpu.make_async_copy(x, y, sems.at[i]) for i, (x, y) in enumerate(moves)]
    for copy in copies:
        copy.start()
    for copy in copies:
        copy.wait()


def edges(value, cot):
    width = value.shape[1]
    return pl.pallas_call(
        edges_kernel,
        out_shape=[kept((k * HALO, width), value.dtype) for k in (1, 2, 4, 3)],
        in_specs=[ANY] * 2,
        out_specs=[VMEM] * 4,
        scratch_shapes=[pltpu.SemaphoreType.DMA((7,))],
        compiler_params=LIMIT,
        name="edges",
    )(*far(value, cot))


def silu_adjoint(mixed, upstream):
    squashed = jax.nn.sigmoid(mixed)
    return upstream * squashed * (1.0 + mixed * (1.0 - squashed))


def tap_sum(taps_ref, lanes, read, first):
    total = first
    for tap in range(4):
        term = taps_ref[tap : tap + 1, lanes] * read(3 * tap)
        total = term if total is None else total + term
    return total


def gate_rows(gate_ref, block):
    return jnp.broadcast_to(gate_ref[pl.ds(block, 1), :], (LANES, LANES)).T


def adjoint_kernel(
    tab_ref, cot_far, value_far, gate_ref, taps_ref, weight_ref, after_ref, scaled, packed,
    cot_ref, value_ref, value_pad, grad_pad, sems, cot_sems, value_sems, *, heads, head_dim, tabs
):
    length, width = cot_ref.shape
    piece = length // PIECES
    loads = []
    for index in range(PIECES):
        part = pl.ds(index * piece, piece)
        for source, target, own in (
            (value_far, value_ref, value_sems), (cot_far, cot_ref, cot_sems)
        ):
            loads.append(pltpu.make_async_copy(source.at[part], target.at[part], own.at[index]))
            loads[-1].start()
    copies = weight_copies(
        tab_ref, weight_ref, packed, sems, [(0, SMALL)], tabs, heads, head_dim
    )
    for copy in copies:
        copy.start()
    strips = width // LANES
    rows = LANES
    for strip in range(strips):
        value_pad[strip, :HALO] = jnp.zeros((HALO, LANES), jnp.float32)
        grad_pad[strip, length:] = jnp.zeros((HALO, LANES), jnp.float32)

    def first(block, carry):
        start = pl.multiple_of(block * rows, rows)
        for strip in range(strips):
            lanes = slice(strip * LANES, (strip + 1) * LANES)
            value_pad[strip, pl.ds(start + HALO, rows)] = value_ref[
                pl.ds(start, rows), lanes
            ].astype(jnp.float32)
            upstream = cot_ref[pl.ds(start, rows), lanes].astype(jnp.float32)
            mixed = tap_sum(
                taps_ref, lanes, lambda back: value_pad[strip, pl.ds(start + HALO - back, rows)], None
            )
            grad_pad[strip, pl.ds(start, rows)] = silu_adjoint(mixed, upstream)
        return carry

    for index in range(PIECES):
        loads[2 * index].wait()
        loads[2 * index + 1].wait()
        lax.fori_loop(index * (piece // rows), (index + 1) * (piece // rows), first, 0)

    def second(block, carry):
        start = pl.multiple_of(block * rows, rows)
        gate = gate_rows(gate_ref, block)
        for strip in range(strips):
            lanes = slice(strip * LANES, (strip + 1) * LANES)
            upstream = cot_ref[pl.ds(start, rows), lanes].astype(jnp.float32)
            total = tap_sum(
                taps_ref, lanes, lambda ahead: grad_pad[strip, pl.ds(start + ahead, rows)], upstream
            )
            scaled[pl.ds(start, rows), lanes] = (gate * total).astype(jnp.bfloat16)
        return carry

    lax.fori_loop(0, length // rows, second, 0)
    for copy in copies:
        copy.wait()


def adjoint_inside(tab_index, cot, value, gate, taps, weight, after, heads, head_dim, tabs):
    length, width = cot.shape
    strips = width // LANES
    return pl.pallas_call(
        lambda *refs: adjoint_kernel(*refs, heads=heads, head_dim=head_dim, tabs=tabs),
        out_shape=[
            kept((length, width), jnp.bfloat16),
            kept((tabs * heads * SMALL, width), jnp.bfloat16),
        ],
        in_specs=[SMEM] + [ANY] * 2 + [VMEM] * 2 + [ANY] * 2,
        out_specs=[VMEM] * 2,
        scratch_shapes=[
            pltpu.VMEM((length, width), jnp.bfloat16),
            pltpu.VMEM((length, width), jnp.bfloat16),
            pltpu.VMEM((strips, length + HALO, LANES), jnp.float32),
            pltpu.VMEM((strips, length + HALO, LANES), jnp.float32),
            pltpu.SemaphoreType.DMA((tabs * heads,)),
            pltpu.SemaphoreType.DMA((PIECES,)),
            pltpu.SemaphoreType.DMA((PIECES,)),
        ],
        compiler_params=LIMIT,
        name="adjoint",
    )(tab_index, *far(cot, value, gate, taps, weight), after)


def finish_kernel(
    inside_ref, packed, prior_ref, next_ref, value_ref, cot_ref, gate_ref, taps_ref,
    scaled, own_ref, one_ref, two_ref, three_ref, window, grads
):
    length, width = scaled.shape
    strips = width // LANES
    scaled[...] = inside_ref[...]
    for side in range(2):
        gate = gate_rows(gate_ref, side * (length // LANES - 1))
        gate = gate[:HALO] if side == 0 else gate[LANES - HALO :]
        place = slice(0, HALO) if side == 0 else slice(length - HALO, length)
        for strip in range(strips):
            lanes = slice(strip * LANES, (strip + 1) * LANES)
            values = [prior_ref[:, lanes], value_ref[: 2 * HALO, lanes]]
            upstream = cot_ref[: 2 * HALO, lanes]
            if side == 1:
                values = [value_ref[2 * HALO :, lanes], next_ref[:HALO, lanes]]
                upstream = jnp.concatenate(
                    [cot_ref[2 * HALO :, lanes], next_ref[HALO:, lanes]], axis=0
                )
            upstream = upstream.astype(jnp.float32)
            window[side, strip] = jnp.concatenate(values, axis=0).astype(jnp.float32)
            mixed = tap_sum(
                taps_ref, lanes,
                lambda back: window[side, strip, HALO - back : 3 * HALO - back], None,
            )
            grads[side, strip] = silu_adjoint(mixed, upstream)
            total = tap_sum(
                taps_ref, lanes, lambda ahead: grads[side, strip, ahead : HALO + ahead],
                upstream[:HALO],
            )
            scaled[place, lanes] = (gate * total).astype(jnp.bfloat16)
    fold = length // 2
    left = lane_below(fold, HALF)
    halves = [
        lax.dot_general(
            scaled[part * fold : (part + 1) * fold], packed[...], ROWS_DIMS,
            preferred_element_type=jnp.float32,
        )
        for part in range(2)
    ]
    outs = [own_ref, one_ref, two_ref, three_ref]
    for tile in range(2):
        lanes = slice(tile * LANES, (tile + 1) * LANES)
        a, b = halves[0][:, lanes], halves[1][:, lanes]
        even = jnp.where(left, a, pltpu.roll(b, HALF, 1))
        odd = jnp.where(left, pltpu.roll(a, HALF, 1), b)
        outs[2 * tile][...] = even.astype(outs[2 * tile].dtype)
        outs[2 * tile + 1][...] = odd.astype(outs[2 * tile + 1].dtype)


def adjoint_terms(inside, packed, halos, gate, taps, tabs):
    length, width = inside.shape
    strips = width // LANES
    folded = (length // 2, LANES)
    return pl.pallas_call(
        finish_kernel,
        out_shape=[kept((length, width), jnp.bfloat16), kept(folded, jnp.float32)]
        + [kept(folded, jnp.bfloat16)] * (tabs - 1),
        in_specs=[VMEM] * 8,
        out_specs=[VMEM] * (tabs + 1),
        scratch_shapes=[
            pltpu.VMEM((2, strips, 3 * HALO, LANES), jnp.float32),
            pltpu.VMEM((2, strips, 2 * HALO, LANES), jnp.float32),
        ],
        compiler_params=LIMIT,
        name="finish",
    )(*near(inside, packed, *halos), gate, taps)


def project_kernel(
    tab_ref, scaled_ref, weight_ref, after_ref, *refs, heads, head_dim, tabs, relatives
):
    *outs, packed, sems = refs
    spans = [(SMALL, WIDE), (SMALL + WIDE, WIDE)]
    copies = weight_copies(
        tab_ref, weight_ref, packed, sems, spans, tabs, heads, head_dim, relatives
    )
    for copy in copies:
        copy.start()
    size = 2 * LANES
    each = len(copies) // len(outs)
    for index, out in enumerate(outs):
        for copy in copies[index * each : (index + 1) * each]:
            copy.wait()
        term = lax.dot_general(
            scaled_ref[...], packed[index * size : (index + 1) * size], ROWS_DIMS,
            preferred_element_type=jnp.float32,
        )
        out[...] = term.astype(out.dtype)


def project(tab_index, scaled, weight, after, heads, head_dim, tabs, relatives, dtype):
    length, width = scaled.shape
    size = (length, 2 * LANES)
    count = len(relatives)
    return pl.pallas_call(
        lambda *refs: project_kernel(
            *refs, heads=heads, head_dim=head_dim, tabs=tabs, relatives=relatives
        ),
        out_shape=[kept(size, dtype)] * count,
        in_specs=[SMEM, VMEM, ANY, ANY],
        out_specs=[VMEM] * count,
        scratch_shapes=[
            pltpu.VMEM((count * 2 * LANES, width), jnp.bfloat16),
            pltpu.SemaphoreType.DMA((count * heads * 2,)),
        ],
        compiler_params=LIMIT,
        name="project",
    )(tab_index, *near(scaled), *far(weight), after)


def sort_tokens(place_ref, grads, ordered, tiles):
    heads, length = place_ref.shape
    rows = 256
    position = lax.broadcasted_iota(jnp.int32, (rows, length), 0)
    for h in range(heads):
        for tile in range(tiles):
            ordered[h, tile, length:] = jnp.zeros((HALF, LANES), jnp.float32)
        for step in range(length // rows):
            chosen = ones_where(place_ref[h : h + 1] - step * rows == position)
            got = jnp.dot(chosen, grads[...], preferred_element_type=jnp.float32)
            for tile in range(tiles):
                ordered[h, tile, step * rows : (step + 1) * rows] = got[
                    :, tile * LANES : (tile + 1) * LANES
                ]


def summed(refs, index):
    total = refs[0][index]
    for ref in refs[1:]:
        total = total + ref[index].astype(jnp.float32)
    return total


def send_small_kernel(
    start_ref, place_ref, meta_ref, own_ref, one_ref, two_ref, three_ref, out_ref, grads, ordered
):
    peers = out_ref.shape[0]
    fold = own_ref.shape[0]
    wide_left = lane_below(fold, HALF)
    total = summed([own_ref, one_ref, two_ref, three_ref], slice(None))
    turned = pltpu.roll(total, HALF, 1)
    grads[:fold] = jnp.where(wide_left, total, turned).astype(jnp.bfloat16)
    grads[fold:] = jnp.where(wide_left, turned, total).astype(jnp.bfloat16)
    sort_tokens(place_ref, grads, ordered, 1)
    lane = lax.broadcasted_iota(jnp.int32, (SMALL, LANES), 1)
    kind = lax.broadcasted_iota(jnp.int32, (META, LANES), 0)
    unroll = 4

    def body(step, carry):
        for part in range(unroll):
            peer = step * unroll + part
            pieces = []
            for half in range(2):
                for h in range(2):
                    start = start_ref[h, peer] + half * SMALL
                    pieces.append(ordered[h, 0, pl.ds(start, SMALL)])
            block = jnp.where(lane < 32, pieces[0], pieces[1])
            upper = jnp.where(lane < 96, pieces[2], pieces[3])
            block = jnp.where(lane < 64, block, upper)
            out_ref[peer, :SMALL] = block.astype(jnp.bfloat16)
            high = jnp.broadcast_to(meta_ref[pl.ds(peer, 1)], (META, LANES))
            low = jnp.broadcast_to(meta_ref[pl.ds(peers + peer, 1)], (META, LANES))
            digits = jnp.where(kind == 0, high, jnp.where(kind == 1, low, 0.0))
            out_ref[peer, SMALL:] = digits.astype(jnp.bfloat16)
        return carry

    lax.fori_loop(0, peers // unroll, body, 0)


def send_small(starts, places, meta, terms, peers):
    heads, length = places.shape
    return pl.pallas_call(
        send_small_kernel,
        out_shape=kept((peers, SMALL + META, LANES), jnp.bfloat16),
        in_specs=[SMEM] + [VMEM] * 6,
        out_specs=VMEM,
        scratch_shapes=[
            pltpu.VMEM((length, LANES), jnp.bfloat16),
            pltpu.VMEM((heads, 1, length + HALF, LANES), jnp.float32),
        ],
        compiler_params=LIMIT,
        name="send_small",
    )(starts, places, meta, *near(*terms))


def send_wide_kernel(
    start_ref, place_ref, own_ref, one_ref, two_ref, three_ref, after_ref, out_ref, grads, ordered
):
    peers = out_ref.shape[0]
    grads[...] = summed([own_ref, one_ref, two_ref, three_ref], slice(None)).astype(jnp.bfloat16)
    sort_tokens(place_ref, grads, ordered, 2)
    left = lane_below(HALF, HALF)
    unroll = 2

    def body(step, carry):
        for part in range(unroll):
            peer = step * unroll + part
            for tile in range(2):
                a = ordered[0, tile, pl.ds(start_ref[0, peer], HALF)]
                b = ordered[1, tile, pl.ds(start_ref[1, peer], HALF)]
                out_ref[peer, tile * HALF : (tile + 1) * HALF] = jnp.where(left, a, b).astype(
                    jnp.bfloat16
                )
        return carry

    lax.fori_loop(0, peers // unroll, body, 0)


def send_wide(starts, places, terms, after, peers):
    heads, length = places.shape
    return pl.pallas_call(
        send_wide_kernel,
        out_shape=kept((peers, 2 * HALF, LANES), jnp.bfloat16),
        in_specs=[SMEM] + [VMEM] * 5 + [ANY],
        out_specs=VMEM,
        scratch_shapes=[
            pltpu.VMEM((length, 2 * LANES), jnp.bfloat16),
            pltpu.VMEM((heads, 2, length + HALF, LANES), jnp.float32),
        ],
        compiler_params=LIMIT,
        name="send_wide",
    )(starts, places, *near(*terms), after)


def add_small_kernel(got_ref, grad_ref, hits_ref, number_ref, numbers):
    peers = got_ref.shape[0]
    heads, _, rows = grad_ref.shape
    for peer in range(peers):
        digits = got_ref[peer, SMALL:].astype(jnp.float32)
        numbers[peer : peer + 1] = digits[0:1] * float(DIGIT) + digits[1:2] - 1.0
    pairs = peers // 2
    even = numbers[pl.ds(0, pairs, stride=2)]
    odd = numbers[pl.ds(1, pairs, stride=2)]
    left = lane_below(pairs, HALF)
    number_ref[0] = jnp.where(left, even, pltpu.roll(odd, HALF, 1)).astype(jnp.int32)
    number_ref[1] = jnp.where(left, pltpu.roll(even, HALF, 1), odd).astype(jnp.int32)
    row_of = lax.broadcasted_iota(jnp.int32, (rows, LANES), 0)
    keep = lane_below(SMALL, HALF)
    totals = [jnp.zeros((rows, LANES), jnp.float32) for _ in range(heads)]
    group = 4
    for step in range(peers // group):
        parts = []
        for peer in range(step * group, (step + 1) * group):
            block = got_ref[peer, :SMALL].astype(jnp.float32)
            parts.append(jnp.where(keep, block, 1.0))
            parts.append(jnp.where(keep, pltpu.roll(block, HALF, 1), 1.0))
        block = jnp.concatenate(parts, axis=0).astype(jnp.bfloat16)
        for h in range(heads):
            chosen = [
                ones_where(number_ref[h, 2 * step + i : 2 * step + i + 1] == row_of)
                for i in range(group // 2)
            ]
            totals[h] = totals[h] + jnp.dot(
                jnp.concatenate(chosen, axis=1), block, preferred_element_type=jnp.float32
            )
    for h in range(heads):
        turned = totals[h].T
        grad_ref[h] = turned[h * SMALL : (h + 1) * SMALL]
        hits_ref[h] = turned[HALF : HALF + 8]


def add_small(got, heads, rows):
    peers = got.shape[0]
    return pl.pallas_call(
        add_small_kernel,
        out_shape=[
            kept((heads, SMALL, rows), jnp.float32),
            kept((heads, 8, rows), jnp.float32),
            kept((heads, peers // 2, LANES), jnp.int32),
        ],
        scratch_shapes=[pltpu.VMEM((peers, LANES), jnp.float32)],
        compiler_params=LIMIT,
        name="add_small",
    )(*near(got))


def update_kernel(
    got_ref, small_ref, hits_ref, number_ref, table_far, one_far, two_far,
    table_out, one_out, two_out, table_ref, one_ref, two_ref, new_table, new_one, new_two,
    sems, out_sems
):
    loads = [
        pltpu.make_async_copy(source, target, sems.at[index])
        for index, (source, target) in enumerate(
            [(table_far, table_ref), (one_far, one_ref), (two_far, two_ref)]
        )
    ]
    for load in loads:
        load.start()
    peers = got_ref.shape[0]
    heads, head_dim, rows = table_ref.shape
    row_of = lax.broadcasted_iota(jnp.int32, (rows, LANES), 0)
    totals = [jnp.zeros((rows, 2 * LANES), jnp.float32) for _ in range(heads)]
    group = 4
    for step in range(peers // group):
        members = range(step * group, (step + 1) * group)
        block = jnp.concatenate(
            [
                jnp.concatenate([got_ref[peer, :HALF] for peer in members], axis=0),
                jnp.concatenate([got_ref[peer, HALF:] for peer in members], axis=0),
            ],
            axis=1,
        )
        for h in range(heads):
            chosen = [
                ones_where(number_ref[h, 2 * step + i : 2 * step + i + 1] == row_of)
                for i in range(group // 2)
            ]
            totals[h] = totals[h] + jnp.dot(
                jnp.concatenate(chosen, axis=1), block, preferred_element_type=jnp.float32
            )
    for load in loads:
        load.wait()
    left = lane_below(rows, HALF)
    turned = [
        jnp.where(
            left, totals[0][:, t * LANES : (t + 1) * LANES], totals[1][:, t * LANES : (t + 1) * LANES]
        ).T
        for t in range(2)
    ]
    stores = []
    for h in range(heads):
        own = slice(h * HALF, (h + 1) * HALF)
        grad = jnp.concatenate([small_ref[h], turned[0][own], turned[1][own]], axis=0)
        touched = jnp.broadcast_to(hits_ref[h, 0:1] > 0.5, (head_dim, rows))
        old_one, old_two, old_table = one_ref[h], two_ref[h], table_ref[h]
        first = beta_one * old_one + (1.0 - beta_one) * grad
        second = beta_two * old_two + (1.0 - beta_two) * grad * grad
        update = (first / (1.0 - beta_one**adam_steps)) / (
            jnp.sqrt(second / (1.0 - beta_two**adam_steps)) + epsilon
        )
        new_table[h] = jnp.where(touched, old_table - learn_rate * update, old_table)
        new_one[h] = jnp.where(touched, first, old_one)
        new_two[h] = jnp.where(touched, second, old_two)
        for index, (source, target) in enumerate(
            [(new_table, table_out), (new_one, one_out), (new_two, two_out)]
        ):
            stores.append(
                pltpu.make_async_copy(source.at[h], target.at[h], out_sems.at[h, index])
            )
            stores[-1].start()
    for store in stores:
        store.wait()


def updated(got, small, hits, numbers, table, one, two):
    return pl.pallas_call(
        update_kernel,
        out_shape=[whole(table.shape, jnp.float32)] * 3,
        in_specs=[VMEM] * 4 + [ANY] * 3,
        out_specs=[ANY] * 3,
        scratch_shapes=[pltpu.VMEM(table.shape, jnp.float32)] * 6
        + [pltpu.SemaphoreType.DMA((3,)), pltpu.SemaphoreType.DMA((table.shape[0], 3))],
        compiler_params=LIMIT,
        name="update",
    )(*near(got, small, hits, numbers), *far(table, one, two))


def shards(
    cotangent,
    saved_value,
    gate_scale,
    conv_weight,
    value_weight,
    owner_ids,
    local_row,
    row_table,
    moment_one,
    moment_two,
):
    heads, rows, head_dim = row_table.shape
    peers = lax.axis_size("seq")
    tabs = lax.axis_size("tab")
    tab_index = lax.axis_index("tab").astype(jnp.int32).reshape(1)
    prior, following, value_edges, cot_edges = edges(saved_value, cotangent)
    prior = shift_by(prior, "seq", 1, False)
    following = shift_by(following, "seq", -1, False)
    places, starts, meta = plan(jnp.swapaxes(owner_ids, 1, 2), local_row, peers)
    gate = gate_scale.reshape(-1, LANES)
    inside, packed = adjoint_inside(
        tab_index, cotangent, saved_value, gate, conv_weight, value_weight, places, heads,
        head_dim, tabs,
    )
    scaled, *small = adjoint_terms(
        inside, packed, (prior, following, value_edges, cot_edges), gate, conv_weight, tabs
    )
    sizes = (heads, head_dim, tabs)
    wide = [None] + list(
        project(
            tab_index, scaled, value_weight, tab_index, *sizes, range(1, tabs), jnp.bfloat16
        )
    )
    for i in range(1, tabs):
        small[i] = shift_by(small[i], "tab", i, True)
        wide[i] = shift_by(wide[i], "tab", i, True)
    blocks = send_small(starts, places, meta, small, peers)
    got = lax.all_to_all(blocks, "seq", split_axis=0, concat_axis=0, tiled=True)
    wide[:1] = project(
        tab_index, scaled, value_weight, blocks, *sizes, range(1), jnp.float32
    )
    wide_blocks = send_wide(starts, places, wide, blocks, peers)
    wide_got = lax.all_to_all(wide_blocks, "seq", split_axis=0, concat_axis=0, tiled=True)
    small_grad, hits, numbers = add_small(got, heads, rows)
    state = [jnp.swapaxes(x, 1, 2) for x in (row_table, moment_one, moment_two)]
    new = updated(wide_got, small_grad, hits, numbers, *state)
    return tuple(jnp.swapaxes(x, 1, 2) for x in new)


def solution(mesh):
    in_specs = (
        P("seq", "tab"),
        P("seq", "tab"),
        P("seq"),
        P(None, "tab"),
        P(None, "tab"),
        P("tab", "seq", None),
        P("tab", "seq"),
        P("tab", "seq", None),
        P("tab", "seq", None),
        P("tab", "seq", None),
    )
    out_specs = (P("tab", "seq", None), P("tab", "seq", None), P("tab", "seq", None))
    return jax.shard_map(shards, mesh=mesh, in_specs=in_specs, out_specs=out_specs, check_vma=False)
```

```python
import jax
import jax.numpy as jnp
from jax import lax
from jax.experimental import pallas as pl
from jax.experimental.pallas import tpu as pltpu
from jax.sharding import PartitionSpec as P


beta_one = 0.9
beta_two = 0.95
learn_rate = 0.01
adam_steps = 10.0
epsilon = 1e-08

LANES = 128
HALF = 64
HALO = 16
DIGIT = 32
META = 8
PIECES = 4
SMALL = 32
ROWS_DIMS = (((1,), (1,)), ((), ()))
VMEM = pl.BlockSpec(memory_space=pltpu.VMEM)
SMEM = pl.BlockSpec(memory_space=pltpu.SMEM)
ANY = pl.BlockSpec(memory_space=pl.ANY)
LIMIT = pltpu.CompilerParams(vmem_limit_bytes=24 << 20)


def shift_by(block, axis, distance, wrap):
    size = lax.axis_size(axis)
    if wrap:
        route = [(i, (i + distance) % size) for i in range(size)]
    else:
        route = [(i, i + distance) for i in range(size) if 0 <= i + distance < size]
    return lax.ppermute(block, axis, route)


def whole(shape, dtype):
    return jax.ShapeDtypeStruct(shape, dtype)


def kept(shape, dtype):
    return pltpu.VMEM(shape, dtype)


def near(*arrays):
    return [pltpu.with_memory_space_constraint(x, pltpu.VMEM) for x in arrays]


def far(*arrays):
    return [pltpu.with_memory_space_constraint(x, pltpu.HBM) for x in arrays]


def lane_below(rows, bound):
    return lax.broadcasted_iota(jnp.int32, (rows, LANES), 1) < bound


def ones_where(mask):
    return jnp.where(mask, 1.0, 0.0).astype(jnp.bfloat16)


def plan_kernel(owners_ref, row_ref, place_ref, start_ref, meta_ref, rank_ref, *, peers):
    heads, _, length = owners_ref.shape
    owner_of = lax.broadcasted_iota(jnp.int32, (peers, LANES), 0)
    before = lax.broadcasted_iota(jnp.int32, (LANES, 2 * LANES), 0)
    after = lax.broadcasted_iota(jnp.int32, (LANES, 2 * LANES), 1)
    counter = ones_where((before < after) | (after >= LANES))
    carry = jnp.zeros((heads * peers, LANES), jnp.float32)
    for block in range(length // LANES):
        lanes = slice(block * LANES, (block + 1) * LANES)
        named = [
            jnp.where(owners_ref[h, :, lanes] == owner_of, 1.0, 0.0) for h in range(heads)
        ]
        named = jnp.concatenate(named, axis=0)
        counts = jnp.dot(
            named.astype(jnp.bfloat16), counter, preferred_element_type=jnp.float32
        )
        rank = named * (counts[:, :LANES] + carry)
        carry = carry + counts[:, LANES:]
        for h in range(heads):
            own = jnp.sum(rank[h * peers : (h + 1) * peers], axis=0, keepdims=True)
            rank_ref[h : h + 1, lanes] = own
    owner_wide = lax.broadcasted_iota(jnp.int32, (LANES, length), 0)
    column = lax.broadcasted_iota(jnp.int32, (LANES, length), 0)
    total = jnp.zeros((2 * peers, LANES), jnp.float32)
    for h in range(heads):
        owners = owners_ref[h]
        below = ones_where(owners < owner_wide)
        starts = lax.dot_general(
            jnp.ones((8, length), jnp.bfloat16), below, ROWS_DIMS,
            preferred_element_type=jnp.float32,
        )
        start_ref[h : h + 1] = starts[0:1].astype(jnp.int32)
        named = jnp.where(owners == owner_wide[:peers], 1.0, 0.0)
        start = jnp.sum(below[:peers].astype(jnp.float32), axis=1, keepdims=True)
        first = jnp.sum(named * start, axis=0, keepdims=True)
        rank = rank_ref[h : h + 1]
        place_ref[h : h + 1] = (first + rank).astype(jnp.int32)
        number = row_ref[h : h + 1] + 1
        high = (number // DIGIT).astype(jnp.float32)
        low = (number % DIGIT).astype(jnp.float32)
        digits = jnp.concatenate([named * high, named * low], axis=0).astype(jnp.bfloat16)
        chosen = ones_where(rank.astype(jnp.int32) + h * HALF == column)
        total = total + lax.dot_general(
            digits, chosen, ROWS_DIMS, preferred_element_type=jnp.float32
        )
    meta_ref[...] = total


def plan(owners, rows, peers):
    heads, _, length = owners.shape
    return pl.pallas_call(
        lambda *refs: plan_kernel(*refs, peers=peers),
        out_shape=[
            whole((heads, length), jnp.int32),
            whole((heads, LANES), jnp.int32),
            whole((2 * peers, LANES), jnp.float32),
        ],
        scratch_shapes=[pltpu.VMEM((heads, length), jnp.float32)],
        compiler_params=LIMIT,
        name="plan",
    )(*far(owners, rows))


def weight_copies(
    tab_ref, weight_ref, packed, sems, spans, tabs, heads, head_dim, relatives=None
):
    copies = []
    place = 0
    for relative in range(tabs) if relatives is None else relatives:
        base = ((tab_ref[0] + relative) % tabs) * (heads * head_dim)
        for low, count in spans:
            for h in range(heads):
                start = pl.multiple_of(base + (h * head_dim + low), 32)
                copies.append(
                    pltpu.make_async_copy(
                        weight_ref.at[pl.ds(start, count)],
                        packed.at[pl.ds(place, count)],
                        sems.at[len(copies)],
                    )
                )
                place += count
    return copies


def edges_kernel(value_far, cot_far, prior_ref, next_ref, value_ref, cot_ref, sems):
    length = value_far.shape[0]
    head, tail = pl.ds(0, HALO), pl.ds(length - HALO, HALO)
    wide_head, wide_tail = pl.ds(0, 2 * HALO), pl.ds(length - 2 * HALO, 2 * HALO)
    moves = [
        (value_far.at[tail], prior_ref),
        (value_far.at[head], next_ref.at[pl.ds(0, HALO)]),
        (cot_far.at[head], next_ref.at[pl.ds(HALO, HALO)]),
        (value_far.at[wide_head], value_ref.at[pl.ds(0, 2 * HALO)]),
        (value_far.at[wide_tail], value_ref.at[pl.ds(2 * HALO, 2 * HALO)]),
        (cot_far.at[wide_head], cot_ref.at[pl.ds(0, 2 * HALO)]),
        (cot_far.at[tail], cot_ref.at[pl.ds(2 * HALO, HALO)]),
    ]
    copies = [pltpu.make_async_copy(x, y, sems.at[i]) for i, (x, y) in enumerate(moves)]
    for copy in copies:
        copy.start()
    for copy in copies:
        copy.wait()


def edges(value, cot):
    width = value.shape[1]
    return pl.pallas_call(
        edges_kernel,
        out_shape=[kept((k * HALO, width), value.dtype) for k in (1, 2, 4, 3)],
        in_specs=[ANY] * 2,
        out_specs=[VMEM] * 4,
        scratch_shapes=[pltpu.SemaphoreType.DMA((7,))],
        compiler_params=LIMIT,
        name="edges",
    )(*far(value, cot))


def silu_adjoint(mixed, upstream):
    squashed = jax.nn.sigmoid(mixed)
    return upstream * squashed * (1.0 + mixed * (1.0 - squashed))


def tap_sum(taps_ref, lanes, read, first):
    total = first
    for tap in range(4):
        term = taps_ref[tap : tap + 1, lanes] * read(3 * tap)
        total = term if total is None else total + term
    return total


def gate_rows(gate_ref, block):
    return jnp.broadcast_to(gate_ref[pl.ds(block, 1), :], (LANES, LANES)).T


def adjoint_kernel(
    tab_ref, cot_far, value_far, gate_ref, taps_ref, weight_ref, after_ref, scaled, packed,
    cot_ref, value_ref, value_pad, grad_pad, sems, cot_sems, value_sems, *, heads, head_dim, tabs
):
    length, width = cot_ref.shape
    piece = length // PIECES
    loads = []
    for index in range(PIECES):
        part = pl.ds(index * piece, piece)
        for source, target, own in (
            (value_far, value_ref, value_sems), (cot_far, cot_ref, cot_sems)
        ):
            loads.append(pltpu.make_async_copy(source.at[part], target.at[part], own.at[index]))
            loads[-1].start()
    copies = weight_copies(
        tab_ref, weight_ref, packed, sems, [(0, SMALL)], tabs, heads, head_dim
    )
    for copy in copies:
        copy.start()
    strips = width // LANES
    rows = LANES
    for strip in range(strips):
        value_pad[strip, :HALO] = jnp.zeros((HALO, LANES), jnp.float32)
        grad_pad[strip, length:] = jnp.zeros((HALO, LANES), jnp.float32)

    def first(block, carry):
        start = pl.multiple_of(block * rows, rows)
        for strip in range(strips):
            lanes = slice(strip * LANES, (strip + 1) * LANES)
            value_pad[strip, pl.ds(start + HALO, rows)] = value_ref[
                pl.ds(start, rows), lanes
            ].astype(jnp.float32)
            upstream = cot_ref[pl.ds(start, rows), lanes].astype(jnp.float32)
            mixed = tap_sum(
                taps_ref, lanes, lambda back: value_pad[strip, pl.ds(start + HALO - back, rows)], None
            )
            grad_pad[strip, pl.ds(start, rows)] = silu_adjoint(mixed, upstream)
        return carry

    for index in range(PIECES):
        loads[2 * index].wait()
        loads[2 * index + 1].wait()
        lax.fori_loop(index * (piece // rows), (index + 1) * (piece // rows), first, 0)

    def second(block, carry):
        start = pl.multiple_of(block * rows, rows)
        gate = gate_rows(gate_ref, block)
        for strip in range(strips):
            lanes = slice(strip * LANES, (strip + 1) * LANES)
            upstream = cot_ref[pl.ds(start, rows), lanes].astype(jnp.float32)
            total = tap_sum(
                taps_ref, lanes, lambda ahead: grad_pad[strip, pl.ds(start + ahead, rows)], upstream
            )
            scaled[pl.ds(start, rows), lanes] = (gate * total).astype(jnp.bfloat16)
        return carry

    lax.fori_loop(0, length // rows, second, 0)
    for copy in copies:
        copy.wait()


def adjoint_inside(tab_index, cot, value, gate, taps, weight, after, heads, head_dim, tabs):
    length, width = cot.shape
    strips = width // LANES
    return pl.pallas_call(
        lambda *refs: adjoint_kernel(*refs, heads=heads, head_dim=head_dim, tabs=tabs),
        out_shape=[
            kept((length, width), jnp.bfloat16),
            kept((tabs * heads * SMALL, width), jnp.bfloat16),
        ],
        in_specs=[SMEM] + [ANY] * 2 + [VMEM] * 2 + [ANY] * 2,
        out_specs=[VMEM] * 2,
        scratch_shapes=[
            pltpu.VMEM((length, width), jnp.bfloat16),
            pltpu.VMEM((length, width), jnp.bfloat16),
            pltpu.VMEM((strips, length + HALO, LANES), jnp.float32),
            pltpu.VMEM((strips, length + HALO, LANES), jnp.float32),
            pltpu.SemaphoreType.DMA((tabs * heads,)),
            pltpu.SemaphoreType.DMA((PIECES,)),
            pltpu.SemaphoreType.DMA((PIECES,)),
        ],
        compiler_params=LIMIT,
        name="adjoint",
    )(tab_index, *far(cot, value, gate, taps, weight), after)


def finish_kernel(
    inside_ref, packed, prior_ref, next_ref, value_ref, cot_ref, gate_ref, taps_ref,
    scaled, own_ref, one_ref, two_ref, three_ref, window, grads
):
    length, width = scaled.shape
    strips = width // LANES
    scaled[...] = inside_ref[...]
    for side in range(2):
        gate = gate_rows(gate_ref, side * (length // LANES - 1))
        gate = gate[:HALO] if side == 0 else gate[LANES - HALO :]
        place = slice(0, HALO) if side == 0 else slice(length - HALO, length)
        for strip in range(strips):
            lanes = slice(strip * LANES, (strip + 1) * LANES)
            values = [prior_ref[:, lanes], value_ref[: 2 * HALO, lanes]]
            upstream = cot_ref[: 2 * HALO, lanes]
            if side == 1:
                values = [value_ref[2 * HALO :, lanes], next_ref[:HALO, lanes]]
                upstream = jnp.concatenate(
                    [cot_ref[2 * HALO :, lanes], next_ref[HALO:, lanes]], axis=0
                )
            upstream = upstream.astype(jnp.float32)
            window[side, strip] = jnp.concatenate(values, axis=0).astype(jnp.float32)
            mixed = tap_sum(
                taps_ref, lanes,
                lambda back: window[side, strip, HALO - back : 3 * HALO - back], None,
            )
            grads[side, strip] = silu_adjoint(mixed, upstream)
            total = tap_sum(
                taps_ref, lanes, lambda ahead: grads[side, strip, ahead : HALO + ahead],
                upstream[:HALO],
            )
            scaled[place, lanes] = (gate * total).astype(jnp.bfloat16)
    fold = length // 2
    left = lane_below(fold, HALF)
    halves = [
        lax.dot_general(
            scaled[part * fold : (part + 1) * fold], packed[...], ROWS_DIMS,
            preferred_element_type=jnp.float32,
        )
        for part in range(2)
    ]
    outs = [own_ref, one_ref, two_ref, three_ref]
    for tile in range(2):
        lanes = slice(tile * LANES, (tile + 1) * LANES)
        a, b = halves[0][:, lanes], halves[1][:, lanes]
        even = jnp.where(left, a, pltpu.roll(b, HALF, 1))
        odd = jnp.where(left, pltpu.roll(a, HALF, 1), b)
        outs[2 * tile][...] = even.astype(outs[2 * tile].dtype)
        outs[2 * tile + 1][...] = odd.astype(outs[2 * tile + 1].dtype)


def adjoint_terms(inside, packed, halos, gate, taps, tabs):
    length, width = inside.shape
    strips = width // LANES
    folded = (length // 2, LANES)
    return pl.pallas_call(
        finish_kernel,
        out_shape=[kept((length, width), jnp.bfloat16), kept(folded, jnp.float32)]
        + [kept(folded, jnp.bfloat16)] * (tabs - 1),
        in_specs=[VMEM] * 8,
        out_specs=[VMEM] * (tabs + 1),
        scratch_shapes=[
            pltpu.VMEM((2, strips, 3 * HALO, LANES), jnp.float32),
            pltpu.VMEM((2, strips, 2 * HALO, LANES), jnp.float32),
        ],
        compiler_params=LIMIT,
        name="finish",
    )(*near(inside, packed, *halos), gate, taps)


def project_kernel(
    tab_ref, scaled_ref, weight_ref, after_ref, *refs, heads, head_dim, tabs, relatives
):
    *outs, packed, sems = refs
    spans = [(SMALL, LANES)]
    copies = weight_copies(
        tab_ref, weight_ref, packed, sems, spans, tabs, heads, head_dim, relatives
    )
    for copy in copies:
        copy.start()
    size = 2 * LANES
    each = len(copies) // len(outs)
    for index, out in enumerate(outs):
        for copy in copies[index * each : (index + 1) * each]:
            copy.wait()
        term = lax.dot_general(
            scaled_ref[...], packed[index * size : (index + 1) * size], ROWS_DIMS,
            preferred_element_type=jnp.float32,
        )
        out[...] = term.astype(out.dtype)


def project(tab_index, scaled, weight, after, heads, head_dim, tabs, relatives, dtype):
    length, width = scaled.shape
    size = (length, 2 * LANES)
    count = len(relatives)
    return pl.pallas_call(
        lambda *refs: project_kernel(
            *refs, heads=heads, head_dim=head_dim, tabs=tabs, relatives=relatives
        ),
        out_shape=[kept(size, dtype)] * count,
        in_specs=[SMEM, VMEM, ANY, ANY],
        out_specs=[VMEM] * count,
        scratch_shapes=[
            pltpu.VMEM((count * 2 * LANES, width), jnp.bfloat16),
            pltpu.SemaphoreType.DMA((count * heads * 2,)),
        ],
        compiler_params=LIMIT,
        name="project",
    )(tab_index, *near(scaled), *far(weight), after)


def sort_tokens(place_ref, grads, ordered, tiles):
    heads, length = place_ref.shape
    rows = 256
    position = lax.broadcasted_iota(jnp.int32, (rows, length), 0)
    for h in range(heads):
        for tile in range(tiles):
            ordered[h, tile, length:] = jnp.zeros((HALF, LANES), jnp.float32)
        for step in range(length // rows):
            chosen = ones_where(place_ref[h : h + 1] - step * rows == position)
            got = jnp.dot(chosen, grads[...], preferred_element_type=jnp.float32)
            for tile in range(tiles):
                ordered[h, tile, step * rows : (step + 1) * rows] = got[
                    :, tile * LANES : (tile + 1) * LANES
                ]


def summed(refs, index):
    total = refs[0][index]
    for ref in refs[1:]:
        total = total + ref[index].astype(jnp.float32)
    return total


def send_small_kernel(
    start_ref, place_ref, meta_ref, own_ref, one_ref, two_ref, three_ref, out_ref, grads, ordered
):
    peers = out_ref.shape[0]
    fold = own_ref.shape[0]
    wide_left = lane_below(fold, HALF)
    total = summed([own_ref, one_ref, two_ref, three_ref], slice(None))
    turned = pltpu.roll(total, HALF, 1)
    grads[:fold] = jnp.where(wide_left, total, turned).astype(jnp.bfloat16)
    grads[fold:] = jnp.where(wide_left, turned, total).astype(jnp.bfloat16)
    sort_tokens(place_ref, grads, ordered, 1)
    lane = lax.broadcasted_iota(jnp.int32, (SMALL, LANES), 1)
    kind = lax.broadcasted_iota(jnp.int32, (META, LANES), 0)
    unroll = 4

    def body(step, carry):
        for part in range(unroll):
            peer = step * unroll + part
            pieces = []
            for half in range(2):
                for h in range(2):
                    start = start_ref[h, peer] + half * SMALL
                    pieces.append(ordered[h, 0, pl.ds(start, SMALL)])
            block = jnp.where(lane < 32, pieces[0], pieces[1])
            upper = jnp.where(lane < 96, pieces[2], pieces[3])
            block = jnp.where(lane < 64, block, upper)
            out_ref[peer, :SMALL] = block.astype(jnp.bfloat16)
            high = jnp.broadcast_to(meta_ref[pl.ds(peer, 1)], (META, LANES))
            low = jnp.broadcast_to(meta_ref[pl.ds(peers + peer, 1)], (META, LANES))
            digits = jnp.where(kind == 0, high, jnp.where(kind == 1, low, 0.0))
            out_ref[peer, SMALL:] = digits.astype(jnp.bfloat16)
        return carry

    lax.fori_loop(0, peers // unroll, body, 0)


def send_small(starts, places, meta, terms, peers):
    heads, length = places.shape
    return pl.pallas_call(
        send_small_kernel,
        out_shape=whole((peers, SMALL + META, LANES), jnp.bfloat16),
        in_specs=[SMEM] + [VMEM] * 6,
        out_specs=VMEM,
        scratch_shapes=[
            pltpu.VMEM((length, LANES), jnp.bfloat16),
            pltpu.VMEM((heads, 1, length + HALF, LANES), jnp.float32),
        ],
        compiler_params=LIMIT,
        name="send_small",
    )(starts, places, meta, *near(*terms))


def send_wide_kernel(
    start_ref, place_ref, own_ref, one_ref, two_ref, three_ref, after_ref, out_ref, grads, ordered
):
    peers = out_ref.shape[0]
    grads[...] = summed([own_ref, one_ref, two_ref, three_ref], slice(None)).astype(jnp.bfloat16)
    sort_tokens(place_ref, grads, ordered, 2)
    unroll = 2

    def body(step, carry):
        for part in range(unroll):
            peer = step * unroll + part
            for h in range(2):
                window = ordered[h, h, pl.ds(start_ref[h, peer], HALF)]
                out_ref[peer, h * HALF : (h + 1) * HALF] = window.astype(jnp.bfloat16)
        return carry

    lax.fori_loop(0, peers // unroll, body, 0)


def send_wide(starts, places, terms, after, peers):
    heads, length = places.shape
    return pl.pallas_call(
        send_wide_kernel,
        out_shape=whole((peers, 2 * HALF, LANES), jnp.bfloat16),
        in_specs=[SMEM] + [VMEM] * 5 + [ANY],
        out_specs=VMEM,
        scratch_shapes=[
            pltpu.VMEM((length, 2 * LANES), jnp.bfloat16),
            pltpu.VMEM((heads, 2, length + HALF, LANES), jnp.float32),
        ],
        compiler_params=LIMIT,
        name="send_wide",
    )(starts, places, *near(*terms), after)


def add_small_kernel(got_ref, grad_ref, hits_ref, low_ref, column_ref, numbers, number_ref):
    peers = got_ref.shape[0]
    heads, _, rows = grad_ref.shape
    for peer in range(peers):
        digits = got_ref[peer, SMALL:].astype(jnp.float32)
        numbers[peer : peer + 1] = digits[0:1] * float(DIGIT) + digits[1:2] - 1.0
    pairs = peers // 2
    even = numbers[pl.ds(0, pairs, stride=2)]
    odd = numbers[pl.ds(1, pairs, stride=2)]
    left = lane_below(pairs, HALF)
    number_ref[0] = jnp.where(left, even, pltpu.roll(odd, HALF, 1)).astype(jnp.int32)
    number_ref[1] = jnp.where(left, pltpu.roll(even, HALF, 1), odd).astype(jnp.int32)
    half = rows // 2
    upper = []
    for h in range(heads):
        number = number_ref[h]
        low_ref[h] = jnp.where(number >= half, number - half, number)
        upper.append(jnp.where(number >= half, 1.0, 0.0))
    upper.append(jnp.zeros((LANES - heads * pairs, LANES), jnp.float32))
    column_ref[...] = jnp.concatenate(upper, axis=0).T
    row_of = lax.broadcasted_iota(jnp.int32, (rows, LANES), 0)
    keep = lane_below(SMALL, HALF)
    totals = [jnp.zeros((rows, LANES), jnp.float32) for _ in range(heads)]
    group = 4
    for step in range(peers // group):
        parts = []
        for peer in range(step * group, (step + 1) * group):
            block = got_ref[peer, :SMALL].astype(jnp.float32)
            parts.append(jnp.where(keep, block, 1.0))
            parts.append(jnp.where(keep, pltpu.roll(block, HALF, 1), 1.0))
        block = jnp.concatenate(parts, axis=0).astype(jnp.bfloat16)
        for h in range(heads):
            chosen = [
                ones_where(number_ref[h, 2 * step + i : 2 * step + i + 1] == row_of)
                for i in range(group // 2)
            ]
            totals[h] = totals[h] + jnp.dot(
                jnp.concatenate(chosen, axis=1), block, preferred_element_type=jnp.float32
            )
    for h in range(heads):
        turned = totals[h].T
        grad_ref[h] = turned[h * SMALL : (h + 1) * SMALL]
        hits_ref[h] = turned[HALF : HALF + 8]


def add_small(got, heads, rows):
    peers = got.shape[0]
    return pl.pallas_call(
        add_small_kernel,
        out_shape=[
            kept((heads, SMALL, rows), jnp.float32),
            kept((heads, 8, rows), jnp.float32),
            kept((heads, peers // 2, LANES), jnp.int32),
            kept((LANES, LANES), jnp.float32),
        ],
        scratch_shapes=[
            pltpu.VMEM((peers, LANES), jnp.float32),
            pltpu.VMEM((heads, peers // 2, LANES), jnp.int32),
        ],
        compiler_params=LIMIT,
        name="add_small",
    )(*near(got))


def update_kernel(
    got_ref, small_ref, hits_ref, low_ref, column_ref, table_far, one_far, two_far,
    table_out, one_out, two_out, table_ref, one_ref, two_ref, new_table, new_one, new_two,
    sems, out_sems
):
    loads = [
        pltpu.make_async_copy(source, target, sems.at[index])
        for index, (source, target) in enumerate(
            [(table_far, table_ref), (one_far, one_ref), (two_far, two_ref)]
        )
    ]
    for load in loads:
        load.start()
    peers = got_ref.shape[0]
    heads, head_dim, rows = table_ref.shape
    half = rows // 2
    row_of = lax.broadcasted_iota(jnp.int32, (half, LANES), 0)
    totals = [jnp.zeros((half, 2 * LANES), jnp.float32) for _ in range(heads)]
    group = 4
    for step in range(peers // group):
        for h in range(heads):
            block = jnp.concatenate(
                [
                    got_ref[peer, h * HALF : (h + 1) * HALF]
                    for peer in range(step * group, (step + 1) * group)
                ],
                axis=0,
            )
            pairs = range(step * group // 2, (step + 1) * group // 2)
            first = h * (peers // 2)
            mask = [
                jnp.broadcast_to(column_ref[:, first + pair : first + pair + 1], (LANES, LANES))
                for pair in pairs
            ]
            upper = block * jnp.concatenate(mask, axis=0).astype(jnp.bfloat16)
            block = jnp.concatenate([block - upper, upper], axis=1)
            chosen = [
                ones_where(low_ref[h, pair : pair + 1] == row_of)
                for pair in range(step * group // 2, (step + 1) * group // 2)
            ]
            totals[h] = totals[h] + jnp.dot(
                jnp.concatenate(chosen, axis=1), block, preferred_element_type=jnp.float32
            )
    for load in loads:
        load.wait()
    stores = []
    for h in range(heads):
        turned = jnp.concatenate([totals[h][:, :LANES].T, totals[h][:, LANES:].T], axis=1)
        grad = jnp.concatenate([small_ref[h], turned], axis=0)
        touched = jnp.broadcast_to(hits_ref[h, 0:1] > 0.5, (head_dim, rows))
        old_one, old_two, old_table = one_ref[h], two_ref[h], table_ref[h]
        first = beta_one * old_one + (1.0 - beta_one) * grad
        second = beta_two * old_two + (1.0 - beta_two) * grad * grad
        update = (first / (1.0 - beta_one**adam_steps)) / (
            jnp.sqrt(second / (1.0 - beta_two**adam_steps)) + epsilon
        )
        new_table[h] = jnp.where(touched, old_table - learn_rate * update, old_table)
        new_one[h] = jnp.where(touched, first, old_one)
        new_two[h] = jnp.where(touched, second, old_two)
        for index, (source, target) in enumerate(
            [(new_table, table_out), (new_one, one_out), (new_two, two_out)]
        ):
            stores.append(
                pltpu.make_async_copy(source.at[h], target.at[h], out_sems.at[h, index])
            )
            stores[-1].start()
    for store in stores:
        store.wait()


def updated(got, small, hits, lows, masks, table, one, two):
    return pl.pallas_call(
        update_kernel,
        out_shape=[whole(table.shape, jnp.float32)] * 3,
        in_specs=[VMEM] * 5 + [ANY] * 3,
        out_specs=[ANY] * 3,
        scratch_shapes=[pltpu.VMEM(table.shape, jnp.float32)] * 6
        + [pltpu.SemaphoreType.DMA((3,)), pltpu.SemaphoreType.DMA((table.shape[0], 3))],
        compiler_params=LIMIT,
        name="update",
    )(*near(got, small, hits, lows, masks), *far(table, one, two))


def shards(
    cotangent,
    saved_value,
    gate_scale,
    conv_weight,
    value_weight,
    owner_ids,
    local_row,
    row_table,
    moment_one,
    moment_two,
):
    heads, rows, head_dim = row_table.shape
    peers = lax.axis_size("seq")
    tabs = lax.axis_size("tab")
    tab_index = lax.axis_index("tab").astype(jnp.int32).reshape(1)
    prior, following, value_edges, cot_edges = edges(saved_value, cotangent)
    prior = shift_by(prior, "seq", 1, False)
    following = shift_by(following, "seq", -1, False)
    places, starts, meta = plan(jnp.swapaxes(owner_ids, 1, 2), local_row, peers)
    gate = gate_scale.reshape(-1, LANES)
    inside, packed = adjoint_inside(
        tab_index, cotangent, saved_value, gate, conv_weight, value_weight, places, heads,
        head_dim, tabs,
    )
    scaled, *small = adjoint_terms(
        inside, packed, (prior, following, value_edges, cot_edges), gate, conv_weight, tabs
    )
    sizes = (heads, head_dim, tabs)
    wide = [None] + list(
        project(
            tab_index, scaled, value_weight, tab_index, *sizes, range(1, tabs), jnp.bfloat16
        )
    )
    for i in range(1, tabs):
        small[i] = shift_by(small[i], "tab", i, True)
        wide[i] = shift_by(wide[i], "tab", i, True)
    blocks = send_small(starts, places, meta, small, peers)
    got = lax.all_to_all(blocks, "seq", split_axis=0, concat_axis=0, tiled=True)
    wide[:1] = project(
        tab_index, scaled, value_weight, blocks, *sizes, range(1), jnp.float32
    )
    wide_blocks = send_wide(starts, places, wide, blocks, peers)
    wide_got = lax.all_to_all(wide_blocks, "seq", split_axis=0, concat_axis=0, tiled=True)
    small_grad, hits, lows, masks = add_small(got, heads, rows)
    state = [jnp.swapaxes(x, 1, 2) for x in (row_table, moment_one, moment_two)]
    new = updated(wide_got, small_grad, hits, lows, masks, *state)
    return tuple(jnp.swapaxes(x, 1, 2) for x in new)


def solution(mesh):
    in_specs = (
        P("seq", "tab"),
        P("seq", "tab"),
        P("seq"),
        P(None, "tab"),
        P(None, "tab"),
        P("tab", "seq", None),
        P("tab", "seq"),
        P("tab", "seq", None),
        P("tab", "seq", None),
        P("tab", "seq", None),
    )
    out_specs = (P("tab", "seq", None), P("tab", "seq", None), P("tab", "seq", None))
    return jax.shard_map(shards, mesh=mesh, in_specs=in_specs, out_specs=out_specs, check_vma=False)
```
